32 devices in a mesh: dp: 8 (over z, x), chan: 4 (over y, core).
Axes of the slice: x: 2, y: 2, z: 4, core: 2. Of those that a mesh axis runs over, the one named last changes fastest.
Arguments:
- activations: bfloat16 [640, 32768], P('chan', 'dp'), may hold values from -6 to 6
- out_grad: bfloat16 [640, 32768], P('chan', 'dp'), may hold values from -6 to 6
- kernel: bfloat16 [640, 5760], P('chan'), may hold values from -0.078125 to 0.078125
- error_in: float32 [8, 640, 5760], P('dp', 'chan'), may hold values from -6 to 6
- q_prev: float32 [640, 4], P('chan'), may hold values from -6 to 6
Outputs:
- in_grad: bfloat16 [640, 32768], P('chan', 'dp')
- q_factor: float32 [640, 4], P('chan')
- new_error: float32 [8, 640, 5760], P('dp', 'chan')
The draws below stay inside these ranges and needn't reach their ends.
All inputs are finite; a program needn't handle non-finite values.
Results may differ from the reference program's by a relative error of at most 0.001.
Values may be sent and summed in bfloat16 or wider, within the bound.
A program may use at most 128 MiB of HBM per device.

```python
import jax
import jax.numpy as jnp
from jax import lax

C = 640
LAT = 64
RANK = 4
CELLS = 32768
N_DP = 8


def steps_of(own_key, shape, cuts, smallest, largest):
    def one(axis_at, blocks):
        steps = jax.random.uniform(jax.random.fold_in(jax.random.fold_in(own_key, 6), axis_at), (blocks,), jnp.float32, smallest / len(cuts), largest / len(cuts))
        return jnp.repeat(jnp.exp(steps), shape[axis_at] // blocks).reshape((-1,) + (1,) * (len(shape) - axis_at - 1))

    factor_of = one(*cuts[0])
    for cut in cuts[1:]:
        factor_of = factor_of * one(*cut)
    return factor_of


def gaussian(rng, shape, scale, limit, pieces=(), kind=jnp.bfloat16):
    loudness = steps_of(rng, shape, pieces, -0.22, 0.18) if pieces else 1.0
    array = jax.random.normal(rng, shape, jnp.float32) * scale * loudness
    return jnp.minimum(jnp.maximum(array, -limit), limit).astype(kind)


def setup_inputs(seed: int = 0) -> dict:
    keys = jax.random.split(jax.random.key(seed), 6)
    activations = gaussian(keys[0], (C, CELLS), 1.0, 6.0, ((0, 4), (1, 8)))
    out_grad = gaussian(keys[1], (C, CELLS), 1.0, 6.0, ((0, 4), (1, 8)))
    kernel = gaussian(keys[2], (C, 9 * C), (9 * C) ** -0.5, 0.078125, ((0, 4),))
    error_in = gaussian(keys[3], (N_DP, C, 9 * C), 0.5, 6.0, ((0, 8), (1, 4)), jnp.float32)
    q_prev = gaussian(keys[4], (C, RANK), 1.0, 6.0, ((0, 4),), jnp.float32)
    return {"activations": activations, "out_grad": out_grad, "kernel": kernel, "error_in": error_in, "q_prev": q_prev}


def reference(activations, out_grad, kernel, error_in, q_prev):
    hi = lax.Precision.HIGHEST
    act_cells = activations.T
    grad_cells = out_grad.T
    kernel_taps = kernel.reshape(C, 9, C)
    x_pad = jnp.pad(act_cells.reshape(N_DP, LAT, LAT, C), ((0, 0), (1, 1), (1, 1), (0, 0)))
    g_pad = jnp.pad(grad_cells.reshape(N_DP, LAT, LAT, C), ((0, 0), (1, 1), (1, 1), (0, 0)))

    def shard_grad(index):
        zero = jnp.zeros((), jnp.int32)
        x_rows = lax.dynamic_slice(x_pad, (index.astype(jnp.int32), zero, zero, zero), (1, LAT + 2, LAT + 2, C))[0]
        g_rows = lax.dynamic_slice_in_dim(grad_cells, (index * LAT * LAT).astype(jnp.int32), LAT * LAT, 0)
        tap_terms = []
        for tap_index in range(9):
            row_shift, col_shift = divmod(tap_index, 3)
            window = x_rows[row_shift:row_shift + LAT, col_shift:col_shift + LAT].reshape(-1, C)
            tap_terms.append(lax.dot_general(g_rows.astype(jnp.float32), window.astype(jnp.float32), (((0,), (0,)), ((), ())), preferred_element_type=jnp.float32))
        grad_w = jnp.stack(tap_terms, axis=1) * (1.0 / LAT)
        return grad_w.reshape(C, 9 * C) + error_in[index]
    matrices = lax.map(shard_grad, jnp.arange(N_DP, dtype=jnp.int32))
    sketch = jnp.einsum('icm,cr->mr', matrices, q_prev, precision=hi) / N_DP
    gram = jnp.dot(sketch.T, sketch, precision=hi)
    lower = jnp.linalg.cholesky(gram)
    basis = jax.scipy.linalg.solve_triangular(lower, sketch.T, lower=True).T
    q_factor = jnp.einsum('icm,mr->cr', matrices, basis, precision=hi) / N_DP
    new_error = matrices - jnp.dot(q_factor, basis.T, precision=hi)[None]

    def image_grad(g_image):
        total = jnp.zeros((LAT * LAT, C), jnp.float32)
        for tap_index in range(9):
            row_shift, col_shift = divmod(tap_index, 3)
            window = g_image[2 - row_shift:2 - row_shift + LAT, 2 - col_shift:2 - col_shift + LAT].reshape(-1, C)
            total = total + lax.dot_general(window.astype(jnp.float32), kernel_taps[:, tap_index, :].astype(jnp.float32), (((1,), (0,)), ((), ())), preferred_element_type=jnp.float32)
        return total.astype(jnp.bfloat16)
    in_grad = lax.map(image_grad, g_pad).reshape(N_DP * LAT * LAT, C).T
    return (in_grad, q_factor, new_error)
```

```python
import functools

import jax
import jax.numpy as jnp
from jax import lax
from jax.experimental import pallas as pl
from jax.experimental.pallas import tpu as pltpu
from jax.sharding import PartitionSpec as P

TAPS = 9
LANES = 128
SUB = 8
X_PARTS = 4
G_PARTS = 8
GROUP = 8
HI = lax.Precision.HIGHEST
F32 = jnp.float32
BF16 = jnp.bfloat16


def kernel_body(
    dims,
    x_hbm, g_hbm, k_hbm, e_hbm, qt_ref,
    in_grad_ref, qf_ref, n_ref,
    x_all, g_all, stack, e_vm, k_vm, k_send, k_all, kt, v_buf,
    s_buf, s_in, share, share_in, s_full, b_ref, f_buf, wide_q,
    local_sem, xs_y, xr_y, xs_c, xr_c, xs_f, xr_f,
    gs_y, gr_y, gs_c, gr_c, gs_f, gr_f, ks, kr,
    ss, sr, cs, cr, as_, ar, fs, fr, bs, br,
):
    n_dp, n_chan, side, rank, pieces = dims
    ch, cells = x_hbm.shape
    channels = ch * n_chan
    dp = lax.axis_index("dp")
    me = lax.axis_index("chan")
    core = me + 1 - 2 * lax.rem(me, 2)
    far = lax.rem(me + 2, n_chan)
    diag = lax.rem(core + 2, n_chan)
    tiles = channels * TAPS // LANES
    tap_tiles = channels // LANES

    def dp_peer(i):
        return lax.rem(dp + i, n_dp)

    def ch_peer(i):
        return lax.rem(me + i, n_chan)

    barrier = pltpu.get_barrier_semaphore()
    for i in range(1, n_chan):
        pl.semaphore_signal(barrier, inc=1, device_id={"chan": ch_peer(i)}, device_id_type=pl.DeviceIdType.MESH)

    @pl.loop(1, n_dp)
    def _(i):
        pl.semaphore_signal(barrier, inc=1, device_id={"dp": dp_peer(i)}, device_id_type=pl.DeviceIdType.MESH)

    def remote(src, dst, send, recv, where):
        return pltpu.make_async_remote_copy(
            src_ref=src, dst_ref=dst, send_sem=send, recv_sem=recv,
            device_id=where, device_id_type=pl.DeviceIdType.MESH,
        )

    local = [
        pltpu.make_async_copy(g_hbm, g_all.at[me], local_sem.at[0]),
        pltpu.make_async_copy(k_hbm, k_vm, local_sem.at[1]),
        pltpu.make_async_copy(x_hbm, x_all.at[me], local_sem.at[2]),
    ]
    for t in range(TAPS):
        local.append(pltpu.make_async_copy(e_hbm.at[0, :, pl.ds(t * channels, channels)], e_vm.at[t], local_sem.at[3 + t]))
    for c in local:
        c.start()

    pl.semaphore_wait(barrier, n_chan - 1 + n_dp - 1)

    xw = cells // X_PARTS
    gw = cells // G_PARTS

    def part(k, w):
        return pl.ds(pl.multiple_of(k * w, LANES), w)

    def x_copy(kind, k):
        s = part(k, xw)
        if kind == "y":
            return remote(x_hbm.at[:, s], x_all.at[me, :, s], xs_y.at[k], xr_y.at[k], {"chan": far})
        if kind == "c":
            return remote(x_hbm.at[:, s], x_all.at[me, :, s], xs_c.at[k], xr_c.at[k], {"chan": core})
        return remote(x_all.at[far, :, s], x_all.at[far, :, s], xs_f.at[k], xr_f.at[k], {"chan": core})

    def g_copy(kind, k):
        s = part(k, gw)
        if kind == "y":
            return remote(g_hbm.at[:, s], g_all.at[me, :, s], gs_y.at[k], gr_y.at[k], {"chan": far})
        if kind == "c":
            return remote(g_hbm.at[:, s], g_all.at[me, :, s], gs_c.at[k], gr_c.at[k], {"chan": core})
        return remote(g_all.at[far, :, s], g_all.at[far, :, s], gs_f.at[k], gr_f.at[k], {"chan": core})

    x_copy("y", 0).start()
    for k in range(X_PARTS):
        x_copy("c", k).start()

    local[1].wait()
    for j in range(n_chan):
        for t in range(TAPS):
            k_send[j, :, t * ch:(t + 1) * ch] = k_vm[:, t * channels + j * ch:t * channels + (j + 1) * ch]
        k_send[j, :, TAPS * ch:] = jnp.zeros((ch, k_send.shape[2] - TAPS * ch), BF16)

    turn = lax.rem(dp, GROUP)
    first = dp - turn
    quarters = GROUP // 2
    k_width = k_send.shape[2] // quarters
    across = far + (diag - far) * (turn // quarters)
    k_lanes = part(lax.rem(turn, quarters), k_width)

    def k_core():
        return remote(k_send.at[core], k_all.at[me], ks.at[0], kr.at[0], {"chan": core})

    def k_across():
        return remote(k_send.at[across, :, k_lanes], k_all.at[me, :, k_lanes], ks.at[1], kr.at[1], {"chan": across})

    def k_share(i):
        block = k_all.at[across, :, k_lanes]
        return remote(block, block, bs.at[i - 1], br.at[i - 1], {"dp": first + lax.rem(turn + i, GROUP)})

    k_across().start()
    for k in range(1, X_PARTS):
        x_copy("y", k).start()
    k_core().start()
    local[0].wait()
    rows = 16

    @pl.loop(0, ch // rows)
    def _(i):
        at = pl.ds(pl.multiple_of(i * rows, rows), rows)
        src = g_all[me, at, :].astype(F32)
        cell = lax.broadcasted_iota(jnp.int32, (1, cells), 1)
        col = cell % side
        row = cell // side
        for b in range(3):
            if b == 0:
                h = pltpu.roll(jnp.where(col != 0, src, 0.0), cells - 1, 1)
            elif b == 2:
                h = pltpu.roll(jnp.where(col != side - 1, src, 0.0), 1, 1)
            else:
                h = src
            for a in range(3):
                if a == 0:
                    v = pltpu.roll(jnp.where(row != 0, h, 0.0), cells - side, 1)
                elif a == 2:
                    v = pltpu.roll(jnp.where(row != side - 1, h, 0.0), side, 1)
                else:
                    v = h
                stack[3 * a + b, at, :] = v.astype(BF16)

    k_across().wait_recv()
    for i in range(1, GROUP):
        k_share(i).start()
    for k in range(G_PARTS):
        g_copy("c", k).start()
    early = G_PARTS // 2
    for k in range(early):
        g_copy("y", k).start()

    k_all[me] = k_send[me]

    def spread(rows_t):
        pad_c = f_buf.shape[2] - ch
        square = jnp.concatenate([rows_t, jnp.zeros((rows_t.shape[0], pad_c), F32)], axis=1) if pad_c else rows_t
        square = jnp.concatenate([square, jnp.zeros((LANES - rows_t.shape[0], square.shape[1]), F32)], axis=0)
        turned = jnp.transpose(square)[:ch]
        for r in range(rank):
            wide_q[r] = jnp.broadcast_to(turned[:, r:r + 1], (ch, LANES))

    spread(qt_ref[...])
    for a in range(3):
        v_buf[a, :, :LANES] = jnp.zeros((ch, LANES), F32)
        v_buf[a, :, LANES + cells:] = jnp.zeros((ch, LANES), F32)

    local[2].wait()

    @pl.loop(0, X_PARTS)
    def _(k):
        x_copy("y", k).wait_recv()
        x_copy("f", k).start()
        x_copy("c", k).wait_recv()
        x_copy("f", k).wait_recv()
        s = part(k, xw)
        for a in range(3):
            lhs = stack[3 * a:3 * a + 3, :, s].reshape(3 * ch, xw)
            rhs = x_all[:, :, s].reshape(channels, xw)
            out = lax.dot_general(lhs, rhs, (((1,), (1,)), ((), ())), preferred_element_type=F32).reshape(3, ch, channels)

            @pl.when(k == 0)
            def _():
                n_ref[3 * a:3 * a + 3] = out

            @pl.when(k > 0)
            def _():
                n_ref[3 * a:3 * a + 3] += out

    s_buf[tiles // pieces:] = jnp.zeros((n_dp - tiles // pieces, pieces, SUB, LANES), F32)
    for t in range(TAPS):
        local[3 + t].wait()
    for t in range(TAPS):
        for l in range(tap_tiles):
            at = t * tap_tiles + l
            lanes = slice(l * LANES, (l + 1) * LANES)
            value = n_ref[t, :, lanes] * (1.0 / side) + e_vm[t, :, lanes]
            n_ref[t, :, lanes] = value
            sums = [
                jnp.sum(jnp.sum((value * wide_q[r]).reshape(ch // SUB, SUB, LANES), axis=0), axis=0, keepdims=True)
                for r in range(rank)
            ]
            s_buf[at // pieces, at % pieces] = jnp.concatenate(sums + [jnp.zeros((SUB - rank, LANES), F32)], axis=0)

    def s_copy(i):
        peer = dp_peer(i)
        return remote(s_buf.at[peer], s_in.at[dp], ss.at[i - 1], sr.at[i - 1], {"dp": peer})

    @pl.loop(1, n_dp)
    def _(i):
        s_copy(i).start()

    for k in range(early, early + 2):
        g_copy("y", k).start()

    k_core().wait_recv()
    for i in range(1, GROUP):
        k_share(i).wait_recv()
    for i in range(k_all.shape[2] // LANES):
        block = k_all[:, :, i * LANES:(i + 1) * LANES].reshape(channels, LANES)
        kt[i * LANES:(i + 1) * LANES, :] = jnp.transpose(block)

    def forward_g(k):
        g_copy("y", k).wait_recv()
        g_copy("f", k).start()

    def in_grad_part(k):
        g_copy("c", k).wait_recv()
        g_copy("f", k).wait_recv()
        s = part(k, gw)
        col = lax.broadcasted_iota(jnp.int32, (1, gw), 1) % side
        for a in range(3):
            y = lax.dot_general(
                kt[3 * a * ch:(3 * a + 3) * ch, :], g_all[:, :, s].reshape(channels, gw),
                (((1,), (0,)), ((), ())), preferred_element_type=F32,
            )
            left = pltpu.roll(jnp.where(col != 0, y[:ch], 0.0), gw - 1, 1)
            right = pltpu.roll(jnp.where(col != side - 1, y[2 * ch:], 0.0), 1, 1)
            v_buf[a, :, pl.ds(pl.multiple_of(LANES + k * gw, LANES), gw)] = left + y[ch:2 * ch] + right

    def finish_part(k):
        base = k * gw
        wide = gw + LANES
        up = pltpu.roll(v_buf[0, :, pl.ds(pl.multiple_of(base + LANES, LANES), wide)], wide - side, 1)[:, :gw]
        down = pltpu.roll(v_buf[2, :, pl.ds(pl.multiple_of(base, LANES), wide)], wide - (LANES - side), 1)[:, :gw]
        mid = v_buf[1, :, pl.ds(pl.multiple_of(base + LANES, LANES), gw)]
        in_grad_ref[:, part(k, gw)] = (up + mid + down).astype(BF16)

    def run_parts(first, last):
        @pl.loop(first, last)
        def _(k):
            forward_g(k)
            in_grad_part(k)

    run_parts(0, 1)

    @pl.loop(1, n_dp)
    def _(i):
        s_copy(i).wait_recv()

    s_in[dp] = s_buf[dp]
    share[...] = lax.fori_loop(0, n_dp, lambda i, v: v + s_in[i], jnp.zeros(share.shape, F32))

    def c_copy(i):
        return remote(share, share_in.at[me], cs.at[i - 1], cr.at[i - 1], {"chan": ch_peer(i)})

    for i in range(1, n_chan):
        c_copy(i).start()
    share_in[me] = share[...]
    run_parts(1, 2)
    for i in range(1, n_chan):
        c_copy(i).wait_recv()
    total = share_in[0]
    for i in range(1, n_chan):
        total = total + share_in[i]
    s_full[dp] = total * (1.0 / n_dp)

    def a_copy(i):
        return remote(s_full.at[dp], s_full.at[dp], as_.at[i - 1], ar.at[i - 1], {"dp": dp_peer(i)})

    @pl.loop(1, n_dp)
    def _(i):
        a_copy(i).start()

    for k in range(early + 2, G_PARTS):
        g_copy("y", k).start()
    run_parts(2, 3)

    @pl.loop(1, n_dp)
    def _(i):
        a_copy(i).wait_recv()

    cols = [s_full[:, :, r, :] for r in range(rank)]

    def inner(u, v):
        return jnp.sum(u * v).reshape(1, 1, 1)

    gram = {}
    for i in range(rank):
        for j in range(i + 1):
            gram[i, j] = inner(cols[i], cols[j])
    low = {}
    for j in range(rank):
        d = gram[j, j]
        for m in range(j):
            d = d - low[j, m] * low[j, m]
        low[j, j] = jnp.sqrt(d)
        for i in range(j + 1, rank):
            d = gram[i, j]
            for m in range(j):
                d = d - low[i, m] * low[j, m]
            low[i, j] = d / low[j, j]
    base = []
    b_ref[...] = jnp.zeros(b_ref.shape, F32)
    for r in range(rank):
        v = cols[r]
        for m in range(r):
            v = v - low[r, m] * base[m]
        v = v / low[r, r]
        base.append(v)
        b_ref[:, :, r, :] = v

    lane = lax.broadcasted_iota(jnp.int32, (1, LANES), 1)
    half = ch // 4
    blocks = []
    for h in range(ch // half):
        acc = [jnp.zeros((half, LANES), F32) for _ in range(rank)]
        for t in range(TAPS):
            for l in range(tap_tiles):
                at = t * tap_tiles + l
                value = n_ref[t, h * half:(h + 1) * half, l * LANES:(l + 1) * LANES]
                for r in range(rank):
                    acc[r] = acc[r] + value * b_ref[at // pieces, at % pieces, r:r + 1, :]
        block = jnp.zeros((half, LANES), F32)
        for r in range(rank):
            block = jnp.where(lane == r, jnp.sum(acc[r], axis=1, keepdims=True), block)
        blocks.append(block)
    pad_c = f_buf.shape[2] - ch
    if pad_c:
        blocks.append(jnp.zeros((pad_c, LANES), F32))
    f_buf[dp] = jnp.transpose(jnp.concatenate(blocks, axis=0))[:SUB]

    def f_copy(i):
        return remote(f_buf.at[dp], f_buf.at[dp], fs.at[i - 1], fr.at[i - 1], {"dp": dp_peer(i)})

    @pl.loop(1, n_dp)
    def _(i):
        f_copy(i).start()

    run_parts(3, 4)

    @pl.loop(1, n_dp)
    def _(i):
        f_copy(i).wait_recv()

    fsum = lax.fori_loop(0, n_dp, lambda i, v: v + f_buf[i], jnp.zeros(f_buf.shape[1:], F32)) * (1.0 / n_dp)
    qf_ref[...] = fsum[:rank, :ch]
    spread(fsum[:rank, :ch])
    for t in range(TAPS):
        for l in range(tap_tiles):
            at = t * tap_tiles + l
            lanes = slice(l * LANES, (l + 1) * LANES)
            value = n_ref[t, :, lanes]
            for r in range(rank):
                value = value - wide_q[r] * b_ref[at // pieces, at % pieces, r:r + 1, :]
            n_ref[t, :, lanes] = value

    run_parts(4, 5)

    @pl.loop(0, 4)
    def _(k):
        finish_part(k)

    @pl.loop(5, G_PARTS)
    def _(k):
        forward_g(k)
        in_grad_part(k)
        finish_part(k - 1)

    finish_part(G_PARTS - 1)

    @pl.loop(0, X_PARTS)
    def _(k):
        x_copy("y", k).wait_send()
        x_copy("c", k).wait_send()
        x_copy("f", k).wait_send()

    @pl.loop(0, G_PARTS)
    def _(k):
        g_copy("y", k).wait_send()
        g_copy("c", k).wait_send()
        g_copy("f", k).wait_send()

    for i in range(1, n_chan):
        c_copy(i).wait_send()
    k_core().wait_send()
    k_across().wait_send()
    for i in range(1, GROUP):
        k_share(i).wait_send()

    @pl.loop(1, n_dp)
    def _(i):
        s_copy(i).wait_send()
        a_copy(i).wait_send()
        f_copy(i).wait_send()


def write_body(in_grad_vm, qf_vm, n_vm, in_grad_hbm, qf_hbm, err_hbm, sem):
    channels = n_vm.shape[2]
    copies = [
        pltpu.make_async_copy(n_vm.at[t], err_hbm.at[0, :, pl.ds(t * channels, channels)], sem.at[t])
        for t in range(TAPS)
    ]
    copies.append(pltpu.make_async_copy(in_grad_vm, in_grad_hbm, sem.at[TAPS]))
    copies.append(pltpu.make_async_copy(qf_vm, qf_hbm, sem.at[TAPS + 1]))
    for c in copies:
        c.start()
    for c in copies:
        c.wait()


def per_device(activations, out_grad, kernel, error_in, q_prev):
    n_dp = lax.axis_size("dp")
    n_chan = lax.axis_size("chan")
    ch, cells = activations.shape
    channels = kernel.shape[1] // TAPS
    rank = q_prev.shape[1]
    side = round(cells ** 0.5)
    tiles = channels * TAPS // LANES
    pieces = -(-tiles // n_dp)
    kw = -(-TAPS * ch // LANES) * LANES
    fw = -(-ch // LANES) * LANES
    qt = q_prev.T
    dma = pltpu.SemaphoreType.DMA
    anyspace = pl.BlockSpec(memory_space=pl.ANY)
    vmem = pl.BlockSpec(memory_space=pltpu.VMEM)
    held = pl.pallas_call(
        functools.partial(kernel_body, (n_dp, n_chan, side, rank, pieces)),
        out_shape=(
            pltpu.VMEM((ch, cells), BF16),
            pltpu.VMEM((rank, ch), F32),
            pltpu.VMEM((TAPS, ch, channels), F32),
        ),
        in_specs=[anyspace, anyspace, anyspace, anyspace, vmem],
        out_specs=(vmem, vmem, vmem),
        scratch_shapes=[
            pltpu.VMEM((n_chan, ch, cells), BF16),
            pltpu.VMEM((n_chan, ch, cells), BF16),
            pltpu.VMEM((TAPS, ch, cells), BF16),
            pltpu.VMEM((TAPS, ch, channels), F32),
            pltpu.VMEM(kernel.shape, BF16),
            pltpu.VMEM((n_chan, ch, kw), BF16),
            pltpu.VMEM((n_chan, ch, kw), BF16),
            pltpu.VMEM((kw, channels), BF16),
            pltpu.VMEM((3, ch, cells + 2 * LANES), F32),
            pltpu.VMEM((n_dp, pieces, SUB, LANES), F32),
            pltpu.VMEM((n_dp, pieces, SUB, LANES), F32),
            pltpu.VMEM((pieces, SUB, LANES), F32),
            pltpu.VMEM((n_chan, pieces, SUB, LANES), F32),
            pltpu.VMEM((n_dp, pieces, SUB, LANES), F32),
            pltpu.VMEM((n_dp, pieces, SUB, LANES), F32),
            pltpu.VMEM((n_dp, SUB, fw), F32),
            pltpu.VMEM((rank, ch, LANES), F32),
            dma((3 + TAPS,)),
        ]
        + [dma((X_PARTS,))] * 6
        + [dma((G_PARTS,))] * 6
        + [dma((n_chan - 1,))] * 2
        + [dma((n_dp - 1,))] * 2
        + [dma((n_chan - 1,))] * 2
        + [dma((n_dp - 1,))] * 4
        + [dma((GROUP - 1,))] * 2,
        compiler_params=pltpu.CompilerParams(
            collective_id=0, has_side_effects=True, vmem_limit_bytes=56000000
        ),
    )(activations, out_grad, kernel, error_in, qt)
    in_grad, qf_t, new_error = pl.pallas_call(
        write_body,
        out_shape=(
            jax.ShapeDtypeStruct((ch, cells), BF16),
            jax.ShapeDtypeStruct((rank, ch), F32),
            jax.ShapeDtypeStruct(error_in.shape, F32),
        ),
        in_specs=[vmem, vmem, vmem],
        out_specs=(anyspace, anyspace, anyspace),
        scratch_shapes=[dma((TAPS + 2,))],
        compiler_params=pltpu.CompilerParams(vmem_limit_bytes=1000000),
    )(*held)
    return in_grad, qf_t.T, new_error


def solution(mesh):
    in_specs = (
        P("chan", "dp"),
        P("chan", "dp"),
        P("chan", None),
        P("dp", "chan", None),
        P("chan", None),
    )
    out_specs = (P("chan", "dp"), P("chan", None), P("dp", "chan", None))
    return jax.shard_map(
        per_device, mesh=mesh, in_specs=in_specs, out_specs=out_specs, check_vma=False
    )
```

```python
import functools

import jax
import jax.numpy as jnp
from jax import lax
from jax.experimental import pallas as pl
from jax.experimental.pallas import tpu as pltpu
from jax.sharding import PartitionSpec as P

TAPS = 9
LANES = 128
SUB = 8
X_PARTS = 8
G_PARTS = 8
N_FIRST = 1
N_SECOND = 2
N_THIRD = 3
GROUP = 8
HI = lax.Precision.HIGHEST
F32 = jnp.float32
BF16 = jnp.bfloat16


def kernel_body(
    dims,
    x_hbm, g_hbm, k_hbm, e_hbm, qt_ref,
    in_grad_ref, qf_ref, n_ref,
    x_all, g_all, stack, e_vm, k_vm, k_send, k_all, kt, v_buf,
    s_buf, s_in, share, share_in, s_full, b_ref, f_buf, wide_q,
    p_own, p_core, p_half, p_in, p_taps, p_acc, p_wide,
    local_sem, xs_y, xr_y, xs_c, xr_c, xs_f, xr_f,
    gs_y, gr_y, gs_c, gr_c, gs_f, gr_f, ks, kr, ps, pr,
    ss, sr, cs, cr, as_, ar, fs, fr, bs, br,
):
    n_dp, n_chan, side, rank, pieces = dims
    ch, cells = x_hbm.shape
    channels = ch * n_chan
    dp = lax.axis_index("dp")
    me = lax.axis_index("chan")
    core = me + 1 - 2 * lax.rem(me, 2)
    far = lax.rem(me + 2, n_chan)
    diag = lax.rem(core + 2, n_chan)
    tiles = channels * TAPS // LANES
    tap_tiles = channels // LANES

    def dp_peer(i):
        return lax.rem(dp + i, n_dp)

    def ch_peer(i):
        return lax.rem(me + i, n_chan)

    barrier = pltpu.get_barrier_semaphore()
    for i in range(1, n_chan):
        pl.semaphore_signal(barrier, inc=1, device_id={"chan": ch_peer(i)}, device_id_type=pl.DeviceIdType.MESH)

    @pl.loop(1, n_dp)
    def _(i):
        pl.semaphore_signal(barrier, inc=1, device_id={"dp": dp_peer(i)}, device_id_type=pl.DeviceIdType.MESH)

    def remote(src, dst, send, recv, where):
        return pltpu.make_async_remote_copy(
            src_ref=src, dst_ref=dst, send_sem=send, recv_sem=recv,
            device_id=where, device_id_type=pl.DeviceIdType.MESH,
        )

    local = [
        pltpu.make_async_copy(g_hbm, g_all.at[me], local_sem.at[0]),
        pltpu.make_async_copy(k_hbm, k_vm, local_sem.at[1]),
        pltpu.make_async_copy(x_hbm, x_all.at[me], local_sem.at[2]),
    ]
    for t in range(TAPS):
        local.append(pltpu.make_async_copy(e_hbm.at[0, :, pl.ds(t * channels, channels)], e_vm.at[t], local_sem.at[3 + t]))
    for c in local:
        c.start()

    pl.semaphore_wait(barrier, n_chan - 1 + n_dp - 1)

    xw = cells // X_PARTS
    gw = cells // G_PARTS

    def part(k, w):
        return pl.ds(pl.multiple_of(k * w, LANES), w)

    def x_copy(kind, k):
        s = part(k, xw)
        if kind == "y":
            return remote(x_hbm.at[:, s], x_all.at[me, :, s], xs_y.at[k], xr_y.at[k], {"chan": far})
        if kind == "c":
            return remote(x_hbm.at[:, s], x_all.at[me, :, s], xs_c.at[k], xr_c.at[k], {"chan": core})
        return remote(x_all.at[far, :, s], x_all.at[far, :, s], xs_f.at[k], xr_f.at[k], {"chan": core})

    def g_copy(kind, k):
        s = part(k, gw)
        if kind == "y":
            return remote(g_hbm.at[:, s], g_all.at[me, :, s], gs_y.at[k], gr_y.at[k], {"chan": far})
        if kind == "c":
            return remote(g_hbm.at[:, s], g_all.at[me, :, s], gs_c.at[k], gr_c.at[k], {"chan": core})
        return remote(g_all.at[far, :, s], g_all.at[far, :, s], gs_f.at[k], gr_f.at[k], {"chan": core})

    x_copy("y", 0).start()
    for k in range(X_PARTS):
        x_copy("c", k).start()

    def split3(v):
        high = v.astype(BF16)
        rest = v - high.astype(F32)
        mid = rest.astype(BF16)
        low = (rest - mid.astype(F32)).astype(BF16)
        return high, mid, low

    half = cells // 2
    quarter = cells // 4
    parity = lax.rem(me, 2)
    pad_r = jnp.zeros((SUB - rank, ch), F32)
    q_parts = [jnp.concatenate([v.astype(F32), pad_r], axis=0) for v in split3(qt_ref[...])]
    q_rows = jnp.concatenate(q_parts + [jnp.zeros((SUB, ch), F32)], axis=0).astype(BF16)
    local[0].wait()
    p = lax.dot_general(q_rows, g_all[me], (((1,), (0,)), ((), ())), preferred_element_type=F32)
    p = p[:SUB] + p[SUB:2 * SUB] + p[2 * SUB:3 * SUB]
    p_own[:rank, :] = p[:rank, :half]
    p_own[rank:, :] = p[:rank, half:]

    def p_core_copy():
        return remote(p_own, p_core, ps.at[0], pr.at[0], {"chan": core})

    def p_far_copy():
        return remote(p_half, p_in.at[parity], ps.at[1], pr.at[1], {"chan": far})

    def p_diag_copy():
        return remote(p_half, p_in.at[parity], ps.at[2], pr.at[2], {"chan": diag})

    p_core_copy().start()

    def spread(rows_t):
        pad_c = f_buf.shape[2] - ch
        square = jnp.concatenate([rows_t, jnp.zeros((rows_t.shape[0], pad_c), F32)], axis=1) if pad_c else rows_t
        square = jnp.concatenate([square, jnp.zeros((LANES - rows_t.shape[0], square.shape[1]), F32)], axis=0)
        turned = jnp.transpose(square)[:ch]
        for r in range(rank):
            wide_q[r] = jnp.broadcast_to(turned[:, r:r + 1], (ch, LANES))

    spread(qt_ref[...])
    p_core_copy().wait_recv()
    both = p_own[...] + p_core[...]
    p_half[...] = jnp.where(parity == 0, both[:, :quarter], both[:, quarter:])
    p_far_copy().start()
    p_diag_copy().start()
    x_copy("y", 1).start()
    for k in range(G_PARTS):
        g_copy("c", k).start()

    local[1].wait()
    for j in range(n_chan):
        for t in range(TAPS):
            k_send[j, :, t * ch:(t + 1) * ch] = k_vm[:, t * channels + j * ch:t * channels + (j + 1) * ch]
        k_send[j, :, TAPS * ch:] = jnp.zeros((ch, k_send.shape[2] - TAPS * ch), BF16)

    turn = lax.rem(dp, GROUP)
    first = dp - turn
    quarters = GROUP // 2
    lines = GROUP // 2
    line = turn // 2
    pair = lax.rem(turn, 2)
    k_width = k_send.shape[2] // quarters

    def k_piece(ln):
        owner = far + (diag - far) * (ln // (lines // 2))
        return owner, part(lax.rem(2 * ln + pair, quarters), k_width)

    across, k_lanes = k_piece(line)

    def k_core():
        return remote(k_send.at[core], k_all.at[me], ks.at[0], kr.at[0], {"chan": core})

    def k_across():
        return remote(k_send.at[across, :, k_lanes], k_all.at[me, :, k_lanes], ks.at[1], kr.at[1], {"chan": across})

    def k_line(i):
        block = k_all.at[across, :, k_lanes]
        peer = first + 2 * lax.rem(line + i, lines) + pair
        return remote(block, block, bs.at[i - 1], br.at[i - 1], {"dp": peer})

    def k_pair(i):
        owner, lanes = k_piece(lax.rem(line + lines - i, lines))
        block = k_all.at[owner, :, lanes]
        at = lines - 1 + i
        return remote(block, block, bs.at[at], br.at[at], {"dp": first + 2 * line + 1 - pair})

    k_across().start()
    x_copy("y", 2).start()
    k_core().start()
    rows = 16

    @pl.loop(0, ch // rows)
    def _(i):
        at = pl.ds(pl.multiple_of(i * rows, rows), rows)
        src = g_all[me, at, :].astype(F32)
        cell = lax.broadcasted_iota(jnp.int32, (1, cells), 1)
        col = cell % side
        row = cell // side
        for b in range(3):
            if b == 0:
                h = pltpu.roll(jnp.where(col != 0, src, 0.0), cells - 1, 1)
            elif b == 2:
                h = pltpu.roll(jnp.where(col != side - 1, src, 0.0), 1, 1)
            else:
                h = src
            for a in range(3):
                if a == 0:
                    v = pltpu.roll(jnp.where(row != 0, h, 0.0), cells - side, 1)
                elif a == 2:
                    v = pltpu.roll(jnp.where(row != side - 1, h, 0.0), side, 1)
                else:
                    v = h
                stack[3 * a + b, at, :] = v.astype(BF16)

    k_all[me] = k_send[me]

    for a in range(3):
        v_buf[a, :, :LANES] = jnp.zeros((ch, LANES), F32)
        v_buf[a, :, LANES + cells:] = jnp.zeros((ch, LANES), F32)

    s_buf[tiles // pieces:] = jnp.zeros((n_dp - tiles // pieces, pieces, SUB, LANES), F32)
    for t in range(TAPS):
        local[3 + t].wait()
    for t in range(TAPS):
        for l in range(tap_tiles):
            at = t * tap_tiles + l
            value = e_vm[t, :, l * LANES:(l + 1) * LANES]
            sums = [
                jnp.sum(jnp.sum((value * wide_q[r]).reshape(ch // SUB, SUB, LANES), axis=0), axis=0, keepdims=True)
                for r in range(rank)
            ]
            s_buf[at // pieces, at % pieces] = jnp.concatenate(sums + [jnp.zeros((SUB - rank, LANES), F32)], axis=0)

    p_far_copy().wait_recv()
    p_diag_copy().wait_recv()
    both = p_own[...] + p_core[...]
    both = jnp.concatenate([both[:, :quarter] + p_in[0], both[:, quarter:] + p_in[1]], axis=1)
    p = jnp.concatenate([both[:rank], both[rank:]], axis=1)
    cell = lax.broadcasted_iota(jnp.int32, (1, cells), 1)
    col = cell % side
    row = cell // side
    p_taps[TAPS * rank:] = jnp.zeros((p_taps.shape[0] - TAPS * rank, cells), F32)
    for b in range(3):
        if b == 0:
            h = pltpu.roll(jnp.where(col != 0, p, 0.0), cells - 1, 1)
        elif b == 2:
            h = pltpu.roll(jnp.where(col != side - 1, p, 0.0), 1, 1)
        else:
            h = p
        for a in range(3):
            if a == 0:
                v = pltpu.roll(jnp.where(row != 0, h, 0.0), cells - side, 1)
            elif a == 2:
                v = pltpu.roll(jnp.where(row != side - 1, h, 0.0), side, 1)
            else:
                v = h
            t = 3 * a + b
            p_taps[t * rank:(t + 1) * rank, :] = v

    local[2].wait()
    p_rows = p_taps.shape[0]
    p_acc[...] = jnp.zeros(p_acc.shape, F32)

    @pl.loop(0, X_PARTS)
    def _(k):
        s = part(k, xw)
        lhs = jnp.concatenate(split3(p_taps[:, s]), axis=0)
        p_acc[...] += lax.dot_general(lhs, x_all[me, :, s], (((1,), (1,)), ((), ())), preferred_element_type=F32)

    first_sketch = (p_acc[:p_rows] + p_acc[p_rows:2 * p_rows] + p_acc[2 * p_rows:]) * (1.0 / side)
    p_wide[...] = jnp.zeros(p_wide.shape, F32)
    for j in range(n_chan):
        @pl.when(me == j)
        def _():
            for t in range(TAPS):
                p_wide[t, :rank, j * ch:(j + 1) * ch] = first_sketch[t * rank:(t + 1) * rank]

    for t in range(TAPS):
        for l in range(tap_tiles):
            at = t * tap_tiles + l
            s_buf[at // pieces, at % pieces] += p_wide[t, :, l * LANES:(l + 1) * LANES]

    x_copy("y", 3).start()

    def forward_x(k):
        x_copy("y", k).wait_recv()
        x_copy("f", k).start()

    def run_n(first, last):
        @pl.loop(first, last)
        def _(k):
            @pl.when(k + 1 < X_PARTS)
            def _():
                forward_x(k + 1)

            x_copy("c", k).wait_recv()
            x_copy("f", k).wait_recv()
            s = part(k, xw)
            for a in range(3):
                lhs = stack[3 * a:3 * a + 3, :, s].reshape(3 * ch, xw)
                rhs = x_all[:, :, s].reshape(channels, xw)
                out = lax.dot_general(lhs, rhs, (((1,), (1,)), ((), ())), preferred_element_type=F32).reshape(3, ch, channels)

                @pl.when(k == 0)
                def _():
                    n_ref[3 * a:3 * a + 3] = out

                @pl.when(k > 0)
                def _():
                    n_ref[3 * a:3 * a + 3] += out

    def s_copy(i):
        peer = dp_peer(i)
        return remote(s_buf.at[peer], s_in.at[dp], ss.at[i - 1], sr.at[i - 1], {"dp": peer})

    @pl.loop(1, n_dp)
    def _(i):
        s_copy(i).start()

    forward_x(0)
    run_n(0, N_FIRST)
    x_copy("y", 4).start()
    k_across().wait_recv()
    for i in range(1, lines):
        k_line(i).start()
    k_pair(0).start()

    def forward_g(k):
        g_copy("y", k).wait_recv()
        g_copy("f", k).start()

    def in_grad_part(k):
        g_copy("c", k).wait_recv()
        g_copy("f", k).wait_recv()
        s = part(k, gw)
        col = lax.broadcasted_iota(jnp.int32, (1, gw), 1) % side
        for a in range(3):
            y = lax.dot_general(
                kt[3 * a * ch:(3 * a + 3) * ch, :], g_all[:, :, s].reshape(channels, gw),
                (((1,), (0,)), ((), ())), preferred_element_type=F32,
            )
            left = pltpu.roll(jnp.where(col != 0, y[:ch], 0.0), gw - 1, 1)
            right = pltpu.roll(jnp.where(col != side - 1, y[2 * ch:], 0.0), 1, 1)
            v_buf[a, :, pl.ds(pl.multiple_of(LANES + k * gw, LANES), gw)] = left + y[ch:2 * ch] + right

    def finish_part(k):
        base = k * gw
        wide = gw + LANES
        up = pltpu.roll(v_buf[0, :, pl.ds(pl.multiple_of(base + LANES, LANES), wide)], wide - side, 1)[:, :gw]
        down = pltpu.roll(v_buf[2, :, pl.ds(pl.multiple_of(base, LANES), wide)], wide - (LANES - side), 1)[:, :gw]
        mid = v_buf[1, :, pl.ds(pl.multiple_of(base + LANES, LANES), gw)]
        in_grad_ref[:, part(k, gw)] = (up + mid + down).astype(BF16)

    @pl.loop(1, n_dp)
    def _(i):
        s_copy(i).wait_recv()

    s_in[dp] = s_buf[dp]
    share[...] = lax.fori_loop(0, n_dp, lambda i, v: v + s_in[i], jnp.zeros(share.shape, F32))

    def c_copy(i):
        return remote(share, share_in.at[me], cs.at[i - 1], cr.at[i - 1], {"chan": ch_peer(i)})

    for i in range(1, n_chan):
        c_copy(i).start()
    share_in[me] = share[...]
    for k in range(5, X_PARTS):
        x_copy("y", k).start()
    for k in range(G_PARTS):
        g_copy("y", k).start()
    run_n(N_FIRST, N_SECOND)
    for i in range(1, n_chan):
        c_copy(i).wait_recv()
    total = share_in[0]
    for i in range(1, n_chan):
        total = total + share_in[i]
    s_full[dp] = total * (1.0 / n_dp)

    def a_copy(i):
        return remote(s_full.at[dp], s_full.at[dp], as_.at[i - 1], ar.at[i - 1], {"dp": dp_peer(i)})

    @pl.loop(1, n_dp)
    def _(i):
        a_copy(i).start()

    run_n(N_SECOND, N_THIRD)

    @pl.loop(1, n_dp)
    def _(i):
        a_copy(i).wait_recv()

    cols = [s_full[:, :, r, :] for r in range(rank)]

    def inner(u, v):
        return jnp.sum(u * v).reshape(1, 1, 1)

    gram = {}
    for i in range(rank):
        for j in range(i + 1):
            gram[i, j] = inner(cols[i], cols[j])
    low = {}
    for j in range(rank):
        d = gram[j, j]
        for m in range(j):
            d = d - low[j, m] * low[j, m]
        low[j, j] = jnp.sqrt(d)
        for i in range(j + 1, rank):
            d = gram[i, j]
            for m in range(j):
                d = d - low[i, m] * low[j, m]
            low[i, j] = d / low[j, j]
    base = []
    b_ref[...] = jnp.zeros(b_ref.shape, F32)
    for r in range(rank):
        v = cols[r]
        for m in range(r):
            v = v - low[r, m] * base[m]
        v = v / low[r, r]
        base.append(v)
        b_ref[:, :, r, :] = v

    for i in range(1, lines):
        k_line(i).wait_recv()
        k_pair(i).start()
    run_n(N_THIRD, X_PARTS)
    lane = lax.broadcasted_iota(jnp.int32, (1, LANES), 1)
    half = ch // 4
    blocks = []
    for h in range(ch // half):
        acc = [jnp.zeros((half, LANES), F32) for _ in range(rank)]
        for t in range(TAPS):
            for l in range(tap_tiles):
                at = t * tap_tiles + l
                rows_h = slice(h * half, (h + 1) * half)
                lanes = slice(l * LANES, (l + 1) * LANES)
                value = n_ref[t, rows_h, lanes] * (1.0 / side) + e_vm[t, rows_h, lanes]
                n_ref[t, rows_h, lanes] = value
                for r in range(rank):
                    acc[r] = acc[r] + value * b_ref[at // pieces, at % pieces, r:r + 1, :]
        block = jnp.zeros((half, LANES), F32)
        for r in range(rank):
            block = jnp.where(lane == r, jnp.sum(acc[r], axis=1, keepdims=True), block)
        blocks.append(block)
    pad_c = f_buf.shape[2] - ch
    if pad_c:
        blocks.append(jnp.zeros((pad_c, LANES), F32))
    f_buf[dp] = jnp.transpose(jnp.concatenate(blocks, axis=0))[:SUB]

    def f_copy(i):
        return remote(f_buf.at[dp], f_buf.at[dp], fs.at[i - 1], fr.at[i - 1], {"dp": dp_peer(i)})

    @pl.loop(1, n_dp)
    def _(i):
        f_copy(i).start()

    k_core().wait_recv()
    for i in range(lines):
        k_pair(i).wait_recv()
    for i in range(k_all.shape[2] // LANES):
        block = k_all[:, :, i * LANES:(i + 1) * LANES].reshape(channels, LANES)
        kt[i * LANES:(i + 1) * LANES, :] = jnp.transpose(block)

    @pl.loop(1, n_dp)
    def _(i):
        f_copy(i).wait_recv()

    fsum = lax.fori_loop(0, n_dp, lambda i, v: v + f_buf[i], jnp.zeros(f_buf.shape[1:], F32)) * (1.0 / n_dp)
    qf_ref[...] = fsum[:rank, :ch]
    spread(fsum[:rank, :ch])
    for t in range(TAPS):
        for l in range(tap_tiles):
            at = t * tap_tiles + l
            lanes = slice(l * LANES, (l + 1) * LANES)
            value = n_ref[t, :, lanes]
            for r in range(rank):
                value = value - wide_q[r] * b_ref[at // pieces, at % pieces, r:r + 1, :]
            n_ref[t, :, lanes] = value

    forward_g(0)

    @pl.loop(0, G_PARTS)
    def _(k):
        @pl.when(k + 1 < G_PARTS)
        def _():
            forward_g(k + 1)

        in_grad_part(k)

        @pl.when(k > 0)
        def _():
            finish_part(k - 1)

    finish_part(G_PARTS - 1)

    @pl.loop(0, X_PARTS)
    def _(k):
        x_copy("y", k).wait_send()
        x_copy("c", k).wait_send()
        x_copy("f", k).wait_send()

    @pl.loop(0, G_PARTS)
    def _(k):
        g_copy("y", k).wait_send()
        g_copy("c", k).wait_send()
        g_copy("f", k).wait_send()

    for i in range(1, n_chan):
        c_copy(i).wait_send()
    k_core().wait_send()
    k_across().wait_send()
    p_core_copy().wait_send()
    p_far_copy().wait_send()
    p_diag_copy().wait_send()
    for i in range(1, lines):
        k_line(i).wait_send()
    for i in range(lines):
        k_pair(i).wait_send()

    @pl.loop(1, n_dp)
    def _(i):
        s_copy(i).wait_send()
        a_copy(i).wait_send()
        f_copy(i).wait_send()


def write_body(in_grad_vm, qf_vm, n_vm, in_grad_hbm, qf_hbm, err_hbm, sem):
    channels = n_vm.shape[2]
    copies = [
        pltpu.make_async_copy(n_vm.at[t], err_hbm.at[0, :, pl.ds(t * channels, channels)], sem.at[t])
        for t in range(TAPS)
    ]
    copies.append(pltpu.make_async_copy(in_grad_vm, in_grad_hbm, sem.at[TAPS]))
    copies.append(pltpu.make_async_copy(qf_vm, qf_hbm, sem.at[TAPS + 1]))
    for c in copies:
        c.start()
    for c in copies:
        c.wait()


def per_device(activations, out_grad, kernel, error_in, q_prev):
    n_dp = lax.axis_size("dp")
    n_chan = lax.axis_size("chan")
    ch, cells = activations.shape
    channels = kernel.shape[1] // TAPS
    rank = q_prev.shape[1]
    side = round(cells ** 0.5)
    tiles = channels * TAPS // LANES
    pieces = -(-tiles // n_dp)
    kw = -(-TAPS * ch // LANES) * LANES
    fw = -(-ch // LANES) * LANES
    qt = q_prev.T
    p_rows = -(-TAPS * rank // (2 * SUB)) * 2 * SUB
    dma = pltpu.SemaphoreType.DMA
    anyspace = pl.BlockSpec(memory_space=pl.ANY)
    vmem = pl.BlockSpec(memory_space=pltpu.VMEM)
    held = pl.pallas_call(
        functools.partial(kernel_body, (n_dp, n_chan, side, rank, pieces)),
        out_shape=(
            pltpu.VMEM((ch, cells), BF16),
            pltpu.VMEM((rank, ch), F32),
            pltpu.VMEM((TAPS, ch, channels), F32),
        ),
        in_specs=[anyspace, anyspace, anyspace, anyspace, vmem],
        out_specs=(vmem, vmem, vmem),
        scratch_shapes=[
            pltpu.VMEM((n_chan, ch, cells), BF16),
            pltpu.VMEM((n_chan, ch, cells), BF16),
            pltpu.VMEM((TAPS, ch, cells), BF16),
            pltpu.VMEM((TAPS, ch, channels), F32),
            pltpu.VMEM(kernel.shape, BF16),
            pltpu.VMEM((n_chan, ch, kw), BF16),
            pltpu.VMEM((n_chan, ch, kw), BF16),
            pltpu.VMEM((kw, channels), BF16),
            pltpu.VMEM((3, ch, cells + 2 * LANES), F32),
            pltpu.VMEM((n_dp, pieces, SUB, LANES), F32),
            pltpu.VMEM((n_dp, pieces, SUB, LANES), F32),
            pltpu.VMEM((pieces, SUB, LANES), F32),
            pltpu.VMEM((n_chan, pieces, SUB, LANES), F32),
            pltpu.VMEM((n_dp, pieces, SUB, LANES), F32),
            pltpu.VMEM((n_dp, pieces, SUB, LANES), F32),
            pltpu.VMEM((n_dp, SUB, fw), F32),
            pltpu.VMEM((rank, ch, LANES), F32),
            pltpu.VMEM((2 * rank, cells // 2), F32),
            pltpu.VMEM((2 * rank, cells // 2), F32),
            pltpu.VMEM((2 * rank, cells // 4), F32),
            pltpu.VMEM((2, 2 * rank, cells // 4), F32),
            pltpu.VMEM((p_rows, cells), F32),
            pltpu.VMEM((3 * p_rows, ch), F32),
            pltpu.VMEM((TAPS, SUB, channels), F32),
            dma((3 + TAPS,)),
        ]
        + [dma((X_PARTS,))] * 6
        + [dma((G_PARTS,))] * 6
        + [dma((n_chan - 1,))] * 4
        + [dma((n_dp - 1,))] * 2
        + [dma((n_chan - 1,))] * 2
        + [dma((n_dp - 1,))] * 4
        + [dma((GROUP - 1,))] * 2,
        compiler_params=pltpu.CompilerParams(
            collective_id=0, has_side_effects=True, vmem_limit_bytes=56000000
        ),
    )(activations, out_grad, kernel, error_in, qt)
    in_grad, qf_t, new_error = pl.pallas_call(
        write_body,
        out_shape=(
            jax.ShapeDtypeStruct((ch, cells), BF16),
            jax.ShapeDtypeStruct((rank, ch), F32),
            jax.ShapeDtypeStruct(error_in.shape, F32),
        ),
        in_specs=[vmem, vmem, vmem],
        out_specs=(anyspace, anyspace, anyspace),
        scratch_shapes=[dma((TAPS + 2,))],
        compiler_params=pltpu.CompilerParams(vmem_limit_bytes=1000000),
    )(*held)
    return in_grad, qf_t.T, new_error


def solution(mesh):
    in_specs = (
        P("chan", "dp"),
        P("chan", "dp"),
        P("chan", None),
        P("dp", "chan", None),
        P("chan", None),
    )
    out_specs = (P("chan", "dp"), P("chan", None), P("dp", "chan", None))
    return jax.shard_map(
        per_device, mesh=mesh, in_specs=in_specs, out_specs=out_specs, check_vma=False
    )
```

```python
import functools

import jax
import jax.numpy as jnp
from jax import lax
from jax.experimental import pallas as pl
from jax.experimental.pallas import tpu as pltpu
from jax.sharding import PartitionSpec as P

TAPS = 9
LANES = 128
SUB = 8
X_PARTS = 8
G_PARTS = 8
N_FIRST = 1
N_SECOND = 2
N_THIRD = 3
GROUP = 8
HI = lax.Precision.HIGHEST
F32 = jnp.float32
BF16 = jnp.bfloat16


def tap_rows(side, kt, g_cols, v_buf, at):
    ch = v_buf.shape[1]
    gw = g_cols.shape[1]
    col = lax.broadcasted_iota(jnp.int32, (1, gw), 1) % side
    for a in range(3):
        y = lax.dot_general(
            kt[3 * a * ch:(3 * a + 3) * ch, :], g_cols,
            (((1,), (0,)), ((), ())), preferred_element_type=F32,
        )
        left = pltpu.roll(jnp.where(col != 0, y[:ch], 0.0), gw - 1, 1)
        right = pltpu.roll(jnp.where(col != side - 1, y[2 * ch:], 0.0), 1, 1)
        v_buf[a, :, at] = left + y[ch:2 * ch] + right


def finish_cells(side, v_buf, base, gw):
    wide = gw + LANES
    up = pltpu.roll(v_buf[0, :, pl.ds(pl.multiple_of(base + LANES, LANES), wide)], wide - side, 1)[:, :gw]
    down = pltpu.roll(v_buf[2, :, pl.ds(pl.multiple_of(base, LANES), wide)], wide - (LANES - side), 1)[:, :gw]
    mid = v_buf[1, :, pl.ds(pl.multiple_of(base + LANES, LANES), gw)]
    return (up + mid + down).astype(BF16)


def kernel_body(
    dims,
    x_hbm, g_hbm, k_hbm, e_hbm, qt_ref,
    in_grad_ref, qf_ref, n_ref, g_all, kt, v_buf,
    x_all, stack, e_vm, k_vm, k_send, k_all,
    s_buf, s_in, share, share_in, s_full, b_ref, f_buf, wide_q,
    p_own, p_core, p_half, p_in, p_taps, p_acc, p_wide,
    local_sem, xs_y, xr_y, xs_c, xr_c, xs_f, xr_f,
    gs_y, gr_y, gs_c, gr_c, gs_f, gr_f, ks, kr, ps, pr,
    ss, sr, cs, cr, as_, ar, fs, fr, bs, br, here, go,
):
    n_dp, n_chan, side, rank, pieces = dims
    ch, cells = x_hbm.shape
    channels = ch * n_chan
    dp = lax.axis_index("dp")
    me = lax.axis_index("chan")
    core = me + 1 - 2 * lax.rem(me, 2)
    far = lax.rem(me + 2, n_chan)
    diag = lax.rem(core + 2, n_chan)
    tiles = channels * TAPS // LANES
    tap_tiles = channels // LANES
    per = SUB // rank

    def dp_peer(i):
        return lax.rem(dp + i, n_dp)

    def ch_peer(i):
        return lax.rem(me + i, n_chan)

    barrier = pltpu.get_barrier_semaphore()
    root = (dp == 0) & (me == 0)

    for i in range(1, n_chan):
        @pl.when((dp != 0) | (ch_peer(i) != 0))
        def _():
            pl.semaphore_signal(barrier, inc=1, device_id={"chan": ch_peer(i)}, device_id_type=pl.DeviceIdType.MESH)

    @pl.when(dp != 0)
    def _():
        pl.semaphore_signal(barrier, inc=1, device_id={"dp": 0, "chan": 0}, device_id_type=pl.DeviceIdType.MESH)

    def enter_group():
        @pl.when(jnp.logical_not(root))
        def _():
            pl.semaphore_wait(barrier, n_chan - 1)

            @pl.when(dp == 0)
            def _():
                pl.semaphore_signal(here, inc=1, device_id={"chan": 0}, device_id_type=pl.DeviceIdType.MESH)

        @pl.when(root)
        def _():
            pl.semaphore_wait(here, n_chan - 1)

    def release_all():
        @pl.when(root)
        def _():
            pl.semaphore_wait(barrier, n_chan * (n_dp - 1))

            @pl.loop(1, n_dp)
            def _(d):
                for j in range(n_chan):
                    pl.semaphore_signal(go, inc=1, device_id={"dp": d, "chan": j}, device_id_type=pl.DeviceIdType.MESH)

            for j in range(1, n_chan):
                pl.semaphore_signal(go, inc=1, device_id={"chan": j}, device_id_type=pl.DeviceIdType.MESH)

    def enter_all():
        @pl.when(jnp.logical_not(root))
        def _():
            pl.semaphore_wait(go, 1)

    def remote(src, dst, send, recv, where):
        return pltpu.make_async_remote_copy(
            src_ref=src, dst_ref=dst, send_sem=send, recv_sem=recv,
            device_id=where, device_id_type=pl.DeviceIdType.MESH,
        )

    local = [
        pltpu.make_async_copy(g_hbm, g_all.at[me], local_sem.at[0]),
        pltpu.make_async_copy(k_hbm, k_vm, local_sem.at[1]),
        pltpu.make_async_copy(x_hbm, x_all.at[me], local_sem.at[2]),
    ]
    for t in range(TAPS):
        local.append(pltpu.make_async_copy(e_hbm.at[0, :, pl.ds(t * channels, channels)], e_vm.at[t], local_sem.at[3 + t]))
    for c in local:
        c.start()

    enter_group()

    xw = cells // X_PARTS
    gw = cells // G_PARTS

    def part(k, w):
        return pl.ds(pl.multiple_of(k * w, LANES), w)

    def x_copy(kind, k):
        s = part(k, xw)
        if kind == "y":
            return remote(x_hbm.at[:, s], x_all.at[me, :, s], xs_y.at[k], xr_y.at[k], {"chan": far})
        if kind == "c":
            return remote(x_hbm.at[:, s], x_all.at[me, :, s], xs_c.at[k], xr_c.at[k], {"chan": core})
        return remote(x_all.at[far, :, s], x_all.at[far, :, s], xs_f.at[k], xr_f.at[k], {"chan": core})

    def g_copy(kind, k):
        s = part(k, gw)
        if kind == "y":
            return remote(g_hbm.at[:, s], g_all.at[me, :, s], gs_y.at[k], gr_y.at[k], {"chan": far})
        if kind == "c":
            return remote(g_hbm.at[:, s], g_all.at[me, :, s], gs_c.at[k], gr_c.at[k], {"chan": core})
        return remote(g_all.at[far, :, s], g_all.at[far, :, s], gs_f.at[k], gr_f.at[k], {"chan": core})

    x_copy("y", 0).start()
    for k in range(X_PARTS):
        x_copy("c", k).start()

    def split3(v):
        high = v.astype(BF16)
        rest = v - high.astype(F32)
        mid = rest.astype(BF16)
        low = (rest - mid.astype(F32)).astype(BF16)
        return high, mid, low

    half = cells // 2
    quarter = cells // 4
    parity = lax.rem(me, 2)
    pad_r = jnp.zeros((SUB - rank, ch), F32)
    q_parts = [jnp.concatenate([v.astype(F32), pad_r], axis=0) for v in split3(qt_ref[...])]
    q_rows = jnp.concatenate(q_parts + [jnp.zeros((SUB, ch), F32)], axis=0).astype(BF16)
    local[0].wait()
    p = lax.dot_general(q_rows, g_all[me], (((1,), (0,)), ((), ())), preferred_element_type=F32)
    p = p[:SUB] + p[SUB:2 * SUB] + p[2 * SUB:3 * SUB]
    p_own[:rank, :] = p[:rank, :half]
    p_own[rank:, :] = p[:rank, half:]

    def p_core_copy():
        return remote(p_own, p_core, ps.at[0], pr.at[0], {"chan": core})

    def p_far_copy():
        return remote(p_half, p_in.at[parity], ps.at[1], pr.at[1], {"chan": far})

    def p_pass_copy():
        return remote(p_in.at[parity], p_in.at[parity], ps.at[2], pr.at[2], {"chan": core})

    p_core_copy().start()

    def spread(rows_t):
        pad_c = f_buf.shape[2] - ch
        square = jnp.concatenate([rows_t, jnp.zeros((rows_t.shape[0], pad_c), F32)], axis=1) if pad_c else rows_t
        square = jnp.concatenate([square, jnp.zeros((LANES - rows_t.shape[0], square.shape[1]), F32)], axis=0)
        turned = jnp.transpose(square)[:ch]
        for r in range(rank):
            wide_q[r] = jnp.broadcast_to(turned[:, r:r + 1], (ch, LANES))

    spread(qt_ref[...])
    p_core_copy().wait_recv()
    both = p_own[...] + p_core[...]
    p_half[...] = jnp.where(parity == 0, both[:, :quarter], both[:, quarter:])
    p_far_copy().start()
    x_copy("y", 1).start()
    for k in range(G_PARTS):
        g_copy("c", k).start()

    local[1].wait()
    for j in range(n_chan):
        for t in range(TAPS):
            k_send[j, :, t * ch:(t + 1) * ch] = k_vm[:, t * channels + j * ch:t * channels + (j + 1) * ch]
        k_send[j, :, TAPS * ch:] = jnp.zeros((ch, k_send.shape[2] - TAPS * ch), BF16)

    turn = lax.rem(dp, GROUP)
    first = dp - turn
    quarters = GROUP // 2
    lines = GROUP // 2
    line = turn // 2
    pair = lax.rem(turn, 2)
    k_width = k_send.shape[2] // quarters

    def k_piece(ln):
        owner = far + (diag - far) * (ln // (lines // 2))
        return owner, part(lax.rem(2 * ln + pair, quarters), k_width)

    across, k_lanes = k_piece(line)

    def k_core():
        return remote(k_send.at[core], k_all.at[me], ks.at[0], kr.at[0], {"chan": core})

    def k_across():
        return remote(k_send.at[across, :, k_lanes], k_all.at[me, :, k_lanes], ks.at[1], kr.at[1], {"chan": across})

    def k_line(i):
        block = k_all.at[across, :, k_lanes]
        peer = first + 2 * lax.rem(line + i, lines) + pair
        return remote(block, block, bs.at[i - 1], br.at[i - 1], {"dp": peer})

    def k_pair(i):
        owner, lanes = k_piece(lax.rem(line + lines - i, lines))
        block = k_all.at[owner, :, lanes]
        at = lines - 1 + i
        return remote(block, block, bs.at[at], br.at[at], {"dp": first + 2 * line + 1 - pair})

    k_across().start()
    x_copy("y", 2).start()
    k_core().start()
    rows = 16

    @pl.loop(0, ch // rows)
    def _(i):
        at = pl.ds(pl.multiple_of(i * rows, rows), rows)
        src = g_all[me, at, :].astype(F32)
        cell = lax.broadcasted_iota(jnp.int32, (1, cells), 1)
        col = cell % side
        row = cell // side
        for b in range(3):
            if b == 0:
                h = pltpu.roll(jnp.where(col != 0, src, 0.0), cells - 1, 1)
            elif b == 2:
                h = pltpu.roll(jnp.where(col != side - 1, src, 0.0), 1, 1)
            else:
                h = src
            for a in range(3):
                if a == 0:
                    v = pltpu.roll(jnp.where(row != 0, h, 0.0), cells - side, 1)
                elif a == 2:
                    v = pltpu.roll(jnp.where(row != side - 1, h, 0.0), side, 1)
                else:
                    v = h
                stack[3 * a + b, at, :] = v.astype(BF16)

    p_far_copy().wait_recv()
    p_pass_copy().start()
    release_all()
    x_copy("y", 3).start()
    k_all[me] = k_send[me]

    for a in range(3):
        v_buf[a, :, :LANES] = jnp.zeros((ch, LANES), F32)
        v_buf[a, :, LANES + cells:] = jnp.zeros((ch, LANES), F32)

    def place(at):
        piece = at % pieces
        return at // pieces, piece // per, piece % per * rank

    s_buf[...] = jnp.zeros(s_buf.shape, F32)
    for t in range(TAPS):
        local[3 + t].wait()
    for t in range(TAPS):
        for l in range(tap_tiles):
            at = t * tap_tiles + l
            value = e_vm[t, :, l * LANES:(l + 1) * LANES]
            sums = [
                jnp.sum(jnp.sum((value * wide_q[r]).reshape(ch // SUB, SUB, LANES), axis=0), axis=0, keepdims=True)
                for r in range(rank)
            ]
            o, c, r0 = place(at)
            s_buf[o, c, r0:r0 + rank, :] = jnp.concatenate(sums, axis=0)

    p_pass_copy().wait_recv()
    both = p_own[...] + p_core[...]
    both = jnp.concatenate([both[:, :quarter] + p_in[0], both[:, quarter:] + p_in[1]], axis=1)
    p = jnp.concatenate([both[:rank], both[rank:]], axis=1)
    cell = lax.broadcasted_iota(jnp.int32, (1, cells), 1)
    col = cell % side
    row = cell // side
    p_taps[TAPS * rank:] = jnp.zeros((p_taps.shape[0] - TAPS * rank, cells), F32)
    for b in range(3):
        if b == 0:
            h = pltpu.roll(jnp.where(col != 0, p, 0.0), cells - 1, 1)
        elif b == 2:
            h = pltpu.roll(jnp.where(col != side - 1, p, 0.0), 1, 1)
        else:
            h = p
        for a in range(3):
            if a == 0:
                v = pltpu.roll(jnp.where(row != 0, h, 0.0), cells - side, 1)
            elif a == 2:
                v = pltpu.roll(jnp.where(row != side - 1, h, 0.0), side, 1)
            else:
                v = h
            t = 3 * a + b
            p_taps[t * rank:(t + 1) * rank, :] = v

    local[2].wait()
    p_rows = p_taps.shape[0]
    p_acc[...] = jnp.zeros(p_acc.shape, F32)

    @pl.loop(0, X_PARTS)
    def _(k):
        s = part(k, xw)
        lhs = jnp.concatenate(split3(p_taps[:, s]), axis=0)
        p_acc[...] += lax.dot_general(lhs, x_all[me, :, s], (((1,), (1,)), ((), ())), preferred_element_type=F32)

    first_sketch = (p_acc[:p_rows] + p_acc[p_rows:2 * p_rows] + p_acc[2 * p_rows:]) * (1.0 / side)
    p_wide[...] = jnp.zeros(p_wide.shape, F32)
    for j in range(n_chan):
        @pl.when(me == j)
        def _():
            for t in range(TAPS):
                p_wide[t, :rank, j * ch:(j + 1) * ch] = first_sketch[t * rank:(t + 1) * rank]

    for t in range(TAPS):
        for l in range(tap_tiles):
            at = t * tap_tiles + l
            o, c, r0 = place(at)
            s_buf[o, c, r0:r0 + rank, :] += p_wide[t, :rank, l * LANES:(l + 1) * LANES]

    x_copy("y", 4).start()

    def forward_x(k):
        x_copy("y", k).wait_recv()
        x_copy("f", k).start()

    def run_n(first, last):
        @pl.loop(first, last)
        def _(k):
            @pl.when(k + 1 < X_PARTS)
            def _():
                forward_x(k + 1)

            x_copy("c", k).wait_recv()
            x_copy("f", k).wait_recv()
            s = part(k, xw)
            for a in range(3):
                lhs = stack[3 * a:3 * a + 3, :, s].reshape(3 * ch, xw)
                rhs = x_all[:, :, s].reshape(channels, xw)
                out = lax.dot_general(lhs, rhs, (((1,), (1,)), ((), ())), preferred_element_type=F32).reshape(3, ch, channels)

                @pl.when(k == 0)
                def _():
                    n_ref[3 * a:3 * a + 3] = out

                @pl.when(k > 0)
                def _():
                    n_ref[3 * a:3 * a + 3] += out

    def s_copy(i):
        peer = dp_peer(i)
        return remote(s_buf.at[peer], s_in.at[dp], ss.at[i - 1], sr.at[i - 1], {"dp": peer})

    enter_all()

    @pl.loop(1, n_dp)
    def _(i):
        s_copy(i).start()

    forward_x(0)
    run_n(0, N_FIRST)
    x_copy("y", 5).start()
    k_across().wait_recv()
    for i in range(1, lines):
        k_line(i).start()
    k_pair(0).start()

    def forward_g(k):
        g_copy("y", k).wait_recv()
        g_copy("f", k).start()

    def in_grad_arrived(k):
        g_copy("c", k).wait_recv()
        g_copy("f", k).wait_recv()

    def in_grad_part(k):
        in_grad_arrived(k)
        g_cols = g_all[:, :, part(k, gw)].reshape(channels, gw)
        tap_rows(side, kt, g_cols, v_buf, pl.ds(pl.multiple_of(LANES + k * gw, LANES), gw))

    def finish_part(k):
        in_grad_ref[:, part(k, gw)] = finish_cells(side, v_buf, k * gw, gw)

    @pl.loop(1, n_dp)
    def _(i):
        s_copy(i).wait_recv()

    s_in[dp] = s_buf[dp]
    share[...] = lax.fori_loop(0, n_dp, lambda i, v: v + s_in[i], jnp.zeros(share.shape, F32))

    def c_copy(i):
        return remote(share, share_in.at[me], cs.at[i - 1], cr.at[i - 1], {"chan": ch_peer(i)})

    for i in range(1, n_chan):
        c_copy(i).start()
    share_in[me] = share[...]
    for k in range(6, X_PARTS):
        x_copy("y", k).start()
    for k in range(G_PARTS):
        g_copy("y", k).start()
    run_n(N_FIRST, N_SECOND)
    for i in range(1, n_chan):
        c_copy(i).wait_recv()
    total = share_in[0]
    for i in range(1, n_chan):
        total = total + share_in[i]
    s_full[dp] = total * (1.0 / n_dp)

    def a_copy(i):
        return remote(s_full.at[dp], s_full.at[dp], as_.at[i - 1], ar.at[i - 1], {"dp": dp_peer(i)})

    @pl.loop(1, n_dp)
    def _(i):
        a_copy(i).start()

    run_n(N_SECOND, N_THIRD)

    @pl.loop(1, n_dp)
    def _(i):
        a_copy(i).wait_recv()

    cols = [[s_full[:, :, u * rank + r, :] for u in range(per)] for r in range(rank)]

    def inner(u, v):
        return sum(jnp.sum(x * y).reshape(1, 1, 1) for x, y in zip(u, v))

    gram = {}
    for i in range(rank):
        for j in range(i + 1):
            gram[i, j] = inner(cols[i], cols[j])
    low = {}
    for j in range(rank):
        d = gram[j, j]
        for m in range(j):
            d = d - low[j, m] * low[j, m]
        low[j, j] = jnp.sqrt(d)
        for i in range(j + 1, rank):
            d = gram[i, j]
            for m in range(j):
                d = d - low[i, m] * low[j, m]
            low[i, j] = d / low[j, j]
    base = []
    b_ref[...] = jnp.zeros(b_ref.shape, F32)
    for r in range(rank):
        v = cols[r]
        for m in range(r):
            v = [x - low[r, m] * y for x, y in zip(v, base[m])]
        v = [x / low[r, r] for x in v]
        base.append(v)
        for u in range(per):
            b_ref[:, :, u * rank + r, :] = v[u]

    for i in range(1, lines):
        k_line(i).wait_recv()
        k_pair(i).start()
    run_n(N_THIRD, X_PARTS)
    lane = lax.broadcasted_iota(jnp.int32, (1, LANES), 1)
    half = ch // 4
    blocks = []
    for h in range(ch // half):
        acc = [jnp.zeros((half, LANES), F32) for _ in range(rank)]
        for t in range(TAPS):
            for l in range(tap_tiles):
                at = t * tap_tiles + l
                rows_h = slice(h * half, (h + 1) * half)
                lanes = slice(l * LANES, (l + 1) * LANES)
                value = n_ref[t, rows_h, lanes] * (1.0 / side) + e_vm[t, rows_h, lanes]
                n_ref[t, rows_h, lanes] = value
                o, c, r0 = place(at)
                for r in range(rank):
                    acc[r] = acc[r] + value * b_ref[o, c, r0 + r:r0 + r + 1, :]
        block = jnp.zeros((half, LANES), F32)
        for r in range(rank):
            block = jnp.where(lane == r, jnp.sum(acc[r], axis=1, keepdims=True), block)
        blocks.append(block)
    pad_c = f_buf.shape[2] - ch
    if pad_c:
        blocks.append(jnp.zeros((pad_c, LANES), F32))
    f_buf[dp] = jnp.transpose(jnp.concatenate(blocks, axis=0))[:SUB]

    def f_copy(i):
        return remote(f_buf.at[dp], f_buf.at[dp], fs.at[i - 1], fr.at[i - 1], {"dp": dp_peer(i)})

    @pl.loop(1, n_dp)
    def _(i):
        f_copy(i).start()

    k_core().wait_recv()
    for i in range(lines):
        k_pair(i).wait_recv()
    for i in range(k_all.shape[2] // LANES):
        block = k_all[:, :, i * LANES:(i + 1) * LANES].reshape(channels, LANES)
        kt[i * LANES:(i + 1) * LANES, :] = jnp.transpose(block)

    @pl.loop(1, n_dp)
    def _(i):
        f_copy(i).wait_recv()

    fsum = lax.fori_loop(0, n_dp, lambda i, v: v + f_buf[i], jnp.zeros(f_buf.shape[1:], F32)) * (1.0 / n_dp)
    qf_ref[...] = fsum[:rank, :ch]
    spread(fsum[:rank, :ch])
    for t in range(TAPS):
        for l in range(tap_tiles):
            at = t * tap_tiles + l
            lanes = slice(l * LANES, (l + 1) * LANES)
            value = n_ref[t, :, lanes]
            o, c, r0 = place(at)
            for r in range(rank):
                value = value - wide_q[r] * b_ref[o, c, r0 + r:r0 + r + 1, :]
            n_ref[t, :, lanes] = value

    forward_g(0)

    @pl.loop(0, G_PARTS - 1)
    def _(k):
        forward_g(k + 1)
        in_grad_part(k)

        @pl.when(k > 0)
        def _():
            finish_part(k - 1)

    in_grad_arrived(G_PARTS - 1)

    @pl.loop(0, X_PARTS)
    def _(k):
        x_copy("y", k).wait_send()
        x_copy("c", k).wait_send()
        x_copy("f", k).wait_send()

    @pl.loop(0, G_PARTS)
    def _(k):
        g_copy("y", k).wait_send()
        g_copy("c", k).wait_send()
        g_copy("f", k).wait_send()

    for i in range(1, n_chan):
        c_copy(i).wait_send()
    k_core().wait_send()
    k_across().wait_send()
    p_core_copy().wait_send()
    p_far_copy().wait_send()
    p_pass_copy().wait_send()
    for i in range(1, lines):
        k_line(i).wait_send()
    for i in range(lines):
        k_pair(i).wait_send()

    @pl.loop(1, n_dp)
    def _(i):
        s_copy(i).wait_send()
        a_copy(i).wait_send()
        f_copy(i).wait_send()


def tail_body(side, in_grad_vm, qf_vm, n_vm, g_vm, kt_vm, v_vm, in_grad_hbm, qf_hbm, err_hbm, v_tail, out, sem):
    n_chan, ch, cells = g_vm.shape
    channels = n_vm.shape[2]
    gw = cells // G_PARTS
    done = cells - 2 * gw
    copies = [
        pltpu.make_async_copy(n_vm.at[t], err_hbm.at[0, :, pl.ds(t * channels, channels)], sem.at[t])
        for t in range(TAPS)
    ]
    copies.append(pltpu.make_async_copy(qf_vm, qf_hbm, sem.at[TAPS]))
    copies.append(pltpu.make_async_copy(in_grad_vm, in_grad_hbm.at[:, :done], sem.at[TAPS + 1]))
    for c in copies:
        c.start()
    v_tail[:, :, :LANES + gw] = v_vm[:, :, done:done + LANES + gw]
    v_tail[:, :, LANES + 2 * gw:] = jnp.zeros((3, ch, LANES), F32)
    tap_rows(side, kt_vm, g_vm[:, :, done + gw:].reshape(channels, gw), v_tail, slice(LANES + gw, LANES + 2 * gw))
    for k in range(2):
        out[:, k * gw:(k + 1) * gw] = finish_cells(side, v_tail, k * gw, gw)
    last = pltpu.make_async_copy(out, in_grad_hbm.at[:, done:], sem.at[TAPS + 2])
    last.start()
    for c in copies:
        c.wait()
    last.wait()


def per_device(activations, out_grad, kernel, error_in, q_prev):
    n_dp = lax.axis_size("dp")
    n_chan = lax.axis_size("chan")
    ch, cells = activations.shape
    channels = kernel.shape[1] // TAPS
    rank = q_prev.shape[1]
    side = round(cells ** 0.5)
    gw = cells // G_PARTS
    tiles = channels * TAPS // LANES
    pieces = -(-tiles // n_dp)
    packs = -(-pieces // (SUB // rank))
    kw = -(-TAPS * ch // LANES) * LANES
    fw = -(-ch // LANES) * LANES
    qt = q_prev.T
    p_rows = -(-TAPS * rank // (2 * SUB)) * 2 * SUB
    dma = pltpu.SemaphoreType.DMA
    anyspace = pl.BlockSpec(memory_space=pl.ANY)
    vmem = pl.BlockSpec(memory_space=pltpu.VMEM)
    held = pl.pallas_call(
        functools.partial(kernel_body, (n_dp, n_chan, side, rank, pieces)),
        out_shape=(
            pltpu.VMEM((ch, cells - 2 * gw), BF16),
            pltpu.VMEM((rank, ch), F32),
            pltpu.VMEM((TAPS, ch, channels), F32),
            pltpu.VMEM((n_chan, ch, cells), BF16),
            pltpu.VMEM((kw, channels), BF16),
            pltpu.VMEM((3, ch, cells + 2 * LANES), F32),
        ),
        in_specs=[anyspace, anyspace, anyspace, anyspace, vmem],
        out_specs=(vmem,) * 6,
        scratch_shapes=[
            pltpu.VMEM((n_chan, ch, cells), BF16),
            pltpu.VMEM((TAPS, ch, cells), BF16),
            pltpu.VMEM((TAPS, ch, channels), F32),
            pltpu.VMEM(kernel.shape, BF16),
            pltpu.VMEM((n_chan, ch, kw), BF16),
            pltpu.VMEM((n_chan, ch, kw), BF16),
            pltpu.VMEM((n_dp, packs, SUB, LANES), F32),
            pltpu.VMEM((n_dp, packs, SUB, LANES), F32),
            pltpu.VMEM((packs, SUB, LANES), F32),
            pltpu.VMEM((n_chan, packs, SUB, LANES), F32),
            pltpu.VMEM((n_dp, packs, SUB, LANES), F32),
            pltpu.VMEM((n_dp, packs, SUB, LANES), F32),
            pltpu.VMEM((n_dp, SUB, fw), F32),
            pltpu.VMEM((rank, ch, LANES), F32),
            pltpu.VMEM((2 * rank, cells // 2), F32),
            pltpu.VMEM((2 * rank, cells // 2), F32),
            pltpu.VMEM((2 * rank, cells // 4), F32),
            pltpu.VMEM((2, 2 * rank, cells // 4), F32),
            pltpu.VMEM((p_rows, cells), F32),
            pltpu.VMEM((3 * p_rows, ch), F32),
            pltpu.VMEM((TAPS, SUB, channels), F32),
            dma((3 + TAPS,)),
        ]
        + [dma((X_PARTS,))] * 6
        + [dma((G_PARTS,))] * 6
        + [dma((n_chan - 1,))] * 4
        + [dma((n_dp - 1,))] * 2
        + [dma((n_chan - 1,))] * 2
        + [dma((n_dp - 1,))] * 4
        + [dma((GROUP - 1,))] * 2
        + [pltpu.SemaphoreType.REGULAR] * 2,
        compiler_params=pltpu.CompilerParams(
            collective_id=0, has_side_effects=True, vmem_limit_bytes=42000000
        ),
    )(activations, out_grad, kernel, error_in, qt)
    in_grad, qf_t, new_error = pl.pallas_call(
        functools.partial(tail_body, side),
        out_shape=(
            jax.ShapeDtypeStruct((ch, cells), BF16),
            jax.ShapeDtypeStruct((rank, ch), F32),
            jax.ShapeDtypeStruct(error_in.shape, F32),
        ),
        in_specs=[vmem] * 6,
        out_specs=(anyspace, anyspace, anyspace),
        scratch_shapes=[
            pltpu.VMEM((3, ch, 2 * gw + 2 * LANES), F32),
            pltpu.VMEM((ch, 2 * gw), BF16),
            dma((TAPS + 3,)),
        ],
        compiler_params=pltpu.CompilerParams(vmem_limit_bytes=12000000),
    )(*held)
    return in_grad, qf_t.T, new_error


def solution(mesh):
    in_specs = (
        P("chan", "dp"),
        P("chan", "dp"),
        P("chan", None),
        P("dp", "chan", None),
        P("chan", None),
    )
    out_specs = (P("chan", "dp"), P("chan", None), P("dp", "chan", None))
    return jax.shard_map(
        per_device, mesh=mesh, in_specs=in_specs, out_specs=out_specs, check_vma=False
    )
```

```python
import functools

import jax
import jax.numpy as jnp
from jax import lax
from jax.experimental import pallas as pl
from jax.experimental.pallas import tpu as pltpu
from jax.sharding import PartitionSpec as P

TAPS = 9
LANES = 128
SUB = 8
X_PARTS = 8
G_PARTS = 8
N_FIRST = 1
N_SECOND = 2
N_THIRD = 3
GROUP = 8
G_SPLIT = 3
HI = lax.Precision.HIGHEST
F32 = jnp.float32
BF16 = jnp.bfloat16


def tap_rows(side, kt, g_cols, v_buf, at):
    ch = v_buf.shape[1]
    gw = g_cols.shape[1]
    col = lax.broadcasted_iota(jnp.int32, (1, gw), 1) % side
    for a in range(3):
        y = lax.dot_general(
            kt[3 * a * ch:(3 * a + 3) * ch, :], g_cols,
            (((1,), (0,)), ((), ())), preferred_element_type=F32,
        )
        left = pltpu.roll(jnp.where(col != 0, y[:ch], 0.0), gw - 1, 1)
        right = pltpu.roll(jnp.where(col != side - 1, y[2 * ch:], 0.0), 1, 1)
        v_buf[a, :, at] = left + y[ch:2 * ch] + right


def finish_cells(side, v_buf, base, gw):
    wide = gw + LANES
    up = pltpu.roll(v_buf[0, :, pl.ds(pl.multiple_of(base + LANES, LANES), wide)], wide - side, 1)[:, :gw]
    down = pltpu.roll(v_buf[2, :, pl.ds(pl.multiple_of(base, LANES), wide)], wide - (LANES - side), 1)[:, :gw]
    mid = v_buf[1, :, pl.ds(pl.multiple_of(base + LANES, LANES), gw)]
    return (up + mid + down).astype(BF16)


def kernel_body(
    dims,
    x_hbm, g_hbm, k_hbm, e_hbm, qt_ref,
    in_grad_ref, qf_ref, n_ref, g_all, kt, v_buf,
    x_all, stack, e_vm, k_vm, k_send, k_all,
    s_buf, s_in, share, share_in, s_full, b_ref, f_buf, wide_q,
    p_own, p_core, p_half, p_in, p_taps, p_acc, p_wide,
    local_sem, xs_y, xr_y, xs_c, xr_c, xs_f, xr_f,
    gs_y, gr_y, gs_c, gr_c, gs_f, gr_f, ks, kr, ps, pr,
    ss, sr, cs, cr, as_, ar, fs, fr, bs, br, here, go,
):
    n_dp, n_chan, side, rank, pieces = dims
    ch, cells = x_hbm.shape
    channels = ch * n_chan
    dp = lax.axis_index("dp")
    me = lax.axis_index("chan")
    core = me + 1 - 2 * lax.rem(me, 2)
    far = lax.rem(me + 2, n_chan)
    diag = lax.rem(core + 2, n_chan)
    tiles = channels * TAPS // LANES
    tap_tiles = channels // LANES
    per = SUB // rank

    def dp_peer(i):
        return lax.rem(dp + i, n_dp)

    def ch_peer(i):
        return lax.rem(me + i, n_chan)

    barrier = pltpu.get_barrier_semaphore()
    root = (dp == 0) & (me == 0)

    for i in range(1, n_chan):
        @pl.when((dp != 0) | (ch_peer(i) != 0))
        def _():
            pl.semaphore_signal(barrier, inc=1, device_id={"chan": ch_peer(i)}, device_id_type=pl.DeviceIdType.MESH)

    @pl.when(dp != 0)
    def _():
        pl.semaphore_signal(barrier, inc=1, device_id={"dp": 0, "chan": 0}, device_id_type=pl.DeviceIdType.MESH)

    def enter_group():
        @pl.when(jnp.logical_not(root))
        def _():
            pl.semaphore_wait(barrier, n_chan - 1)

            @pl.when(dp == 0)
            def _():
                pl.semaphore_signal(here, inc=1, device_id={"chan": 0}, device_id_type=pl.DeviceIdType.MESH)

        @pl.when(root)
        def _():
            pl.semaphore_wait(here, n_chan - 1)

    def release_all():
        @pl.when(root)
        def _():
            pl.semaphore_wait(barrier, n_chan * (n_dp - 1))

            @pl.loop(1, n_dp)
            def _(d):
                for j in range(n_chan):
                    pl.semaphore_signal(go, inc=1, device_id={"dp": d, "chan": j}, device_id_type=pl.DeviceIdType.MESH)

            for j in range(1, n_chan):
                pl.semaphore_signal(go, inc=1, device_id={"chan": j}, device_id_type=pl.DeviceIdType.MESH)

    def enter_all():
        @pl.when(jnp.logical_not(root))
        def _():
            pl.semaphore_wait(go, 1)

    def remote(src, dst, send, recv, where):
        return pltpu.make_async_remote_copy(
            src_ref=src, dst_ref=dst, send_sem=send, recv_sem=recv,
            device_id=where, device_id_type=pl.DeviceIdType.MESH,
        )

    local = [
        pltpu.make_async_copy(g_hbm, g_all.at[me], local_sem.at[0]),
        pltpu.make_async_copy(k_hbm, k_vm, local_sem.at[1]),
        pltpu.make_async_copy(x_hbm, x_all.at[me], local_sem.at[2]),
    ]
    for t in range(TAPS):
        local.append(pltpu.make_async_copy(e_hbm.at[0, :, pl.ds(t * channels, channels)], e_vm.at[t], local_sem.at[3 + t]))
    for c in local:
        c.start()

    enter_group()

    xw = cells // X_PARTS
    gw = cells // G_PARTS

    def part(k, w):
        return pl.ds(pl.multiple_of(k * w, LANES), w)

    def x_copy(kind, k):
        s = part(k, xw)
        if kind == "y":
            return remote(x_hbm.at[:, s], x_all.at[me, :, s], xs_y.at[k], xr_y.at[k], {"chan": far})
        if kind == "c":
            return remote(x_hbm.at[:, s], x_all.at[me, :, s], xs_c.at[k], xr_c.at[k], {"chan": core})
        return remote(x_all.at[far, :, s], x_all.at[far, :, s], xs_f.at[k], xr_f.at[k], {"chan": core})

    def g_copy(kind, k, w=gw, at=None):
        s = part(k, w)
        at = k if at is None else at
        if kind == "y":
            return remote(g_hbm.at[:, s], g_all.at[me, :, s], gs_y.at[at], gr_y.at[at], {"chan": far})
        if kind == "c":
            return remote(g_hbm.at[:, s], g_all.at[me, :, s], gs_c.at[at], gr_c.at[at], {"chan": core})
        return remote(g_all.at[far, :, s], g_all.at[far, :, s], gs_f.at[at], gr_f.at[at], {"chan": core})

    def g_tail(kind, j):
        return g_copy(kind, 2 * (G_PARTS - 1) + j, gw // 2, G_PARTS - 1 + j)

    x_copy("y", 0).start()
    for k in range(X_PARTS):
        x_copy("c", k).start()

    def split3(v):
        high = v.astype(BF16)
        rest = v - high.astype(F32)
        mid = rest.astype(BF16)
        low = (rest - mid.astype(F32)).astype(BF16)
        return high, mid, low

    half = cells // 2
    quarter = cells // 4
    parity = lax.rem(me, 2)
    pad_r = jnp.zeros((SUB - rank, ch), F32)
    q_parts = [jnp.concatenate([v.astype(F32), pad_r], axis=0) for v in split3(qt_ref[...])]
    q_rows = jnp.concatenate(q_parts + [jnp.zeros((SUB, ch), F32)], axis=0).astype(BF16)
    local[0].wait()
    p = lax.dot_general(q_rows, g_all[me], (((1,), (0,)), ((), ())), preferred_element_type=F32)
    p = p[:SUB] + p[SUB:2 * SUB] + p[2 * SUB:3 * SUB]
    p_own[:rank, :] = p[:rank, :half]
    p_own[rank:, :] = p[:rank, half:]

    def p_core_copy():
        return remote(p_own, p_core, ps.at[0], pr.at[0], {"chan": core})

    def p_far_copy():
        return remote(p_half, p_in.at[parity], ps.at[1], pr.at[1], {"chan": far})

    def p_pass_copy():
        return remote(p_in.at[parity], p_in.at[parity], ps.at[2], pr.at[2], {"chan": core})

    p_core_copy().start()

    def spread(rows_t):
        pad_c = f_buf.shape[2] - ch
        square = jnp.concatenate([rows_t, jnp.zeros((rows_t.shape[0], pad_c), F32)], axis=1) if pad_c else rows_t
        square = jnp.concatenate([square, jnp.zeros((LANES - rows_t.shape[0], square.shape[1]), F32)], axis=0)
        turned = jnp.transpose(square)[:ch]
        for r in range(rank):
            wide_q[r] = jnp.broadcast_to(turned[:, r:r + 1], (ch, LANES))

    spread(qt_ref[...])
    p_core_copy().wait_recv()
    both = p_own[...] + p_core[...]
    p_half[...] = jnp.where(parity == 0, both[:, :quarter], both[:, quarter:])
    p_far_copy().start()
    x_copy("y", 1).start()
    for k in range(G_PARTS):
        g_copy("c", k).start()

    local[1].wait()
    for j in range(n_chan):
        for t in range(TAPS):
            k_send[j, :, t * ch:(t + 1) * ch] = k_vm[:, t * channels + j * ch:t * channels + (j + 1) * ch]
        k_send[j, :, TAPS * ch:] = jnp.zeros((ch, k_send.shape[2] - TAPS * ch), BF16)

    turn = lax.rem(dp, GROUP)
    first = dp - turn
    quarters = GROUP // 2
    lines = GROUP // 2
    line = turn // 2
    pair = lax.rem(turn, 2)
    k_width = k_send.shape[2] // quarters

    def k_piece(ln):
        owner = far + (diag - far) * (ln // (lines // 2))
        return owner, part(lax.rem(2 * ln + pair, quarters), k_width)

    across, k_lanes = k_piece(line)

    def k_core():
        return remote(k_send.at[core], k_all.at[me], ks.at[0], kr.at[0], {"chan": core})

    def k_across():
        return remote(k_send.at[across, :, k_lanes], k_all.at[me, :, k_lanes], ks.at[1], kr.at[1], {"chan": across})

    def k_line(i):
        block = k_all.at[across, :, k_lanes]
        peer = first + 2 * lax.rem(line + i, lines) + pair
        return remote(block, block, bs.at[i - 1], br.at[i - 1], {"dp": peer})

    def k_pair(i):
        owner, lanes = k_piece(lax.rem(line + lines - i, lines))
        block = k_all.at[owner, :, lanes]
        at = lines - 1 + i
        return remote(block, block, bs.at[at], br.at[at], {"dp": first + 2 * line + 1 - pair})

    k_across().start()
    x_copy("y", 2).start()
    k_core().start()
    rows = 16

    @pl.loop(0, ch // rows)
    def _(i):
        at = pl.ds(pl.multiple_of(i * rows, rows), rows)
        src = g_all[me, at, :].astype(F32)
        cell = lax.broadcasted_iota(jnp.int32, (1, cells), 1)
        col = cell % side
        row = cell // side
        for b in range(3):
            if b == 0:
                h = pltpu.roll(jnp.where(col != 0, src, 0.0), cells - 1, 1)
            elif b == 2:
                h = pltpu.roll(jnp.where(col != side - 1, src, 0.0), 1, 1)
            else:
                h = src
            for a in range(3):
                if a == 0:
                    v = pltpu.roll(jnp.where(row != 0, h, 0.0), cells - side, 1)
                elif a == 2:
                    v = pltpu.roll(jnp.where(row != side - 1, h, 0.0), side, 1)
                else:
                    v = h
                stack[3 * a + b, at, :] = v.astype(BF16)

    p_far_copy().wait_recv()
    p_pass_copy().start()
    release_all()
    x_copy("y", 3).start()
    k_all[me] = k_send[me]

    for a in range(3):
        v_buf[a, :, :LANES] = jnp.zeros((ch, LANES), F32)
        v_buf[a, :, LANES + cells:] = jnp.zeros((ch, LANES), F32)

    def place(at):
        piece = at % pieces
        return at // pieces, piece // per, piece % per * rank

    s_buf[...] = jnp.zeros(s_buf.shape, F32)
    for t in range(TAPS):
        local[3 + t].wait()
    for t in range(TAPS):
        for l in range(tap_tiles):
            at = t * tap_tiles + l
            value = e_vm[t, :, l * LANES:(l + 1) * LANES]
            sums = [
                jnp.sum(jnp.sum((value * wide_q[r]).reshape(ch // SUB, SUB, LANES), axis=0), axis=0, keepdims=True)
                for r in range(rank)
            ]
            o, c, r0 = place(at)
            s_buf[o, c, r0:r0 + rank, :] = jnp.concatenate(sums, axis=0)

    p_pass_copy().wait_recv()
    both = p_own[...] + p_core[...]
    both = jnp.concatenate([both[:, :quarter] + p_in[0], both[:, quarter:] + p_in[1]], axis=1)
    p = jnp.concatenate([both[:rank], both[rank:]], axis=1)
    cell = lax.broadcasted_iota(jnp.int32, (1, cells), 1)
    col = cell % side
    row = cell // side
    p_taps[TAPS * rank:] = jnp.zeros((p_taps.shape[0] - TAPS * rank, cells), F32)
    for b in range(3):
        if b == 0:
            h = pltpu.roll(jnp.where(col != 0, p, 0.0), cells - 1, 1)
        elif b == 2:
            h = pltpu.roll(jnp.where(col != side - 1, p, 0.0), 1, 1)
        else:
            h = p
        for a in range(3):
            if a == 0:
                v = pltpu.roll(jnp.where(row != 0, h, 0.0), cells - side, 1)
            elif a == 2:
                v = pltpu.roll(jnp.where(row != side - 1, h, 0.0), side, 1)
            else:
                v = h
            t = 3 * a + b
            p_taps[t * rank:(t + 1) * rank, :] = v

    local[2].wait()
    p_rows = p_taps.shape[0]
    p_acc[...] = jnp.zeros(p_acc.shape, F32)

    @pl.loop(0, X_PARTS)
    def _(k):
        s = part(k, xw)
        lhs = jnp.concatenate(split3(p_taps[:, s]), axis=0)
        p_acc[...] += lax.dot_general(lhs, x_all[me, :, s], (((1,), (1,)), ((), ())), preferred_element_type=F32)

    first_sketch = (p_acc[:p_rows] + p_acc[p_rows:2 * p_rows] + p_acc[2 * p_rows:]) * (1.0 / side)
    p_wide[...] = jnp.zeros(p_wide.shape, F32)
    for j in range(n_chan):
        @pl.when(me == j)
        def _():
            for t in range(TAPS):
                p_wide[t, :rank, j * ch:(j + 1) * ch] = first_sketch[t * rank:(t + 1) * rank]

    for t in range(TAPS):
        for l in range(tap_tiles):
            at = t * tap_tiles + l
            o, c, r0 = place(at)
            s_buf[o, c, r0:r0 + rank, :] += p_wide[t, :rank, l * LANES:(l + 1) * LANES]

    x_copy("y", 4).start()

    def forward_x(k):
        x_copy("y", k).wait_recv()
        x_copy("f", k).start()

    def run_n(first, last):
        @pl.loop(first, last)
        def _(k):
            @pl.when(k + 1 < X_PARTS)
            def _():
                forward_x(k + 1)

            x_copy("c", k).wait_recv()
            x_copy("f", k).wait_recv()
            s = part(k, xw)
            for a in range(3):
                lhs = stack[3 * a:3 * a + 3, :, s].reshape(3 * ch, xw)
                rhs = x_all[:, :, s].reshape(channels, xw)
                out = lax.dot_general(lhs, rhs, (((1,), (1,)), ((), ())), preferred_element_type=F32).reshape(3, ch, channels)

                @pl.when(k == 0)
                def _():
                    n_ref[3 * a:3 * a + 3] = out

                @pl.when(k > 0)
                def _():
                    n_ref[3 * a:3 * a + 3] += out

    def s_copy(i):
        peer = dp_peer(i)
        return remote(s_buf.at[peer], s_in.at[dp], ss.at[i - 1], sr.at[i - 1], {"dp": peer})

    enter_all()

    @pl.loop(1, n_dp)
    def _(i):
        s_copy(i).start()

    forward_x(0)
    run_n(0, N_FIRST)
    x_copy("y", 5).start()
    k_across().wait_recv()
    for i in range(1, lines):
        k_line(i).start()
    k_pair(0).start()

    def forward_g(k):
        g_copy("y", k).wait_recv()
        g_copy("f", k).start()

    def in_grad_arrived(k):
        g_copy("c", k).wait_recv()
        g_copy("f", k).wait_recv()

    def in_grad_part(k):
        in_grad_arrived(k)
        g_cols = g_all[:, :, part(k, gw)].reshape(channels, gw)
        tap_rows(side, kt, g_cols, v_buf, pl.ds(pl.multiple_of(LANES + k * gw, LANES), gw))

    def finish_part(k):
        in_grad_ref[:, part(k, gw)] = finish_cells(side, v_buf, k * gw, gw)

    def run_parts(begin, end):
        @pl.loop(begin, end)
        def _(k):
            @pl.when(k + 1 < G_PARTS - 1)
            def _():
                forward_g(k + 1)

            @pl.when(k + 1 == G_PARTS - 1)
            def _():
                g_tail("y", 0).wait_recv()
                g_tail("f", 0).start()

            in_grad_part(k)

            @pl.when(k > 0)
            def _():
                finish_part(k - 1)

    @pl.loop(1, n_dp)
    def _(i):
        s_copy(i).wait_recv()

    s_in[dp] = s_buf[dp]
    share[...] = lax.fori_loop(0, n_dp, lambda i, v: v + s_in[i], jnp.zeros(share.shape, F32))

    def c_copy(i):
        return remote(share, share_in.at[me], cs.at[i - 1], cr.at[i - 1], {"chan": ch_peer(i)})

    for i in range(1, n_chan):
        c_copy(i).start()
    share_in[me] = share[...]
    for k in range(6, X_PARTS):
        x_copy("y", k).start()
    for k in range(G_PARTS - 1):
        g_copy("y", k).start()
    for j in range(2):
        g_tail("y", j).start()
    run_n(N_FIRST, N_SECOND)
    for i in range(1, n_chan):
        c_copy(i).wait_recv()
    total = share_in[0]
    for i in range(1, n_chan):
        total = total + share_in[i]
    s_full[dp] = total * (1.0 / n_dp)

    def a_copy(i):
        return remote(s_full.at[dp], s_full.at[dp], as_.at[i - 1], ar.at[i - 1], {"dp": dp_peer(i)})

    @pl.loop(1, n_dp)
    def _(i):
        a_copy(i).start()

    run_n(N_SECOND, N_THIRD)

    @pl.loop(1, n_dp)
    def _(i):
        a_copy(i).wait_recv()

    cols = [[s_full[:, :, u * rank + r, :] for u in range(per)] for r in range(rank)]

    def inner(u, v):
        return sum(jnp.sum(x * y).reshape(1, 1, 1) for x, y in zip(u, v))

    gram = {}
    for i in range(rank):
        for j in range(i + 1):
            gram[i, j] = inner(cols[i], cols[j])
    low = {}
    for j in range(rank):
        d = gram[j, j]
        for m in range(j):
            d = d - low[j, m] * low[j, m]
        low[j, j] = jnp.sqrt(d)
        for i in range(j + 1, rank):
            d = gram[i, j]
            for m in range(j):
                d = d - low[i, m] * low[j, m]
            low[i, j] = d / low[j, j]
    base = []
    b_ref[...] = jnp.zeros(b_ref.shape, F32)
    for r in range(rank):
        v = cols[r]
        for m in range(r):
            v = [x - low[r, m] * y for x, y in zip(v, base[m])]
        v = [x / low[r, r] for x in v]
        base.append(v)
        for u in range(per):
            b_ref[:, :, u * rank + r, :] = v[u]

    for i in range(1, lines):
        k_line(i).wait_recv()
        k_pair(i).start()
    run_n(N_THIRD, X_PARTS)
    lane = lax.broadcasted_iota(jnp.int32, (1, LANES), 1)
    half = ch // 4
    blocks = []
    for h in range(ch // half):
        acc = [jnp.zeros((half, LANES), F32) for _ in range(rank)]
        for t in range(TAPS):
            for l in range(tap_tiles):
                at = t * tap_tiles + l
                rows_h = slice(h * half, (h + 1) * half)
                lanes = slice(l * LANES, (l + 1) * LANES)
                value = n_ref[t, rows_h, lanes] * (1.0 / side) + e_vm[t, rows_h, lanes]
                n_ref[t, rows_h, lanes] = value
                o, c, r0 = place(at)
                for r in range(rank):
                    acc[r] = acc[r] + value * b_ref[o, c, r0 + r:r0 + r + 1, :]
        block = jnp.zeros((half, LANES), F32)
        for r in range(rank):
            block = jnp.where(lane == r, jnp.sum(acc[r], axis=1, keepdims=True), block)
        blocks.append(block)
    pad_c = f_buf.shape[2] - ch
    if pad_c:
        blocks.append(jnp.zeros((pad_c, LANES), F32))
    f_buf[dp] = jnp.transpose(jnp.concatenate(blocks, axis=0))[:SUB]

    def f_copy(i):
        return remote(f_buf.at[dp], f_buf.at[dp], fs.at[i - 1], fr.at[i - 1], {"dp": dp_peer(i)})

    @pl.loop(1, n_dp)
    def _(i):
        f_copy(i).start()

    k_core().wait_recv()
    for i in range(lines):
        k_pair(i).wait_recv()
    for i in range(k_all.shape[2] // LANES):
        block = k_all[:, :, i * LANES:(i + 1) * LANES].reshape(channels, LANES)
        kt[i * LANES:(i + 1) * LANES, :] = jnp.transpose(block)

    forward_g(0)
    run_parts(0, G_SPLIT)

    @pl.loop(1, n_dp)
    def _(i):
        f_copy(i).wait_recv()

    fsum = lax.fori_loop(0, n_dp, lambda i, v: v + f_buf[i], jnp.zeros(f_buf.shape[1:], F32)) * (1.0 / n_dp)
    qf_ref[...] = fsum[:rank, :ch]
    spread(fsum[:rank, :ch])
    for t in range(TAPS):
        for l in range(tap_tiles):
            at = t * tap_tiles + l
            lanes = slice(l * LANES, (l + 1) * LANES)
            value = n_ref[t, :, lanes]
            o, c, r0 = place(at)
            for r in range(rank):
                value = value - wide_q[r] * b_ref[o, c, r0 + r:r0 + r + 1, :]
            n_ref[t, :, lanes] = value

    run_parts(G_SPLIT, G_PARTS - 1)
    g_tail("y", 1).wait_recv()
    g_tail("f", 1).start()
    g_copy("c", G_PARTS - 1).wait_recv()
    g_tail("f", 0).wait_recv()
    a0 = (G_PARTS - 1) * gw
    tw = gw // 2
    tap_rows(side, kt, g_all[:, :, a0:a0 + tw].reshape(channels, tw), v_buf, slice(LANES + a0, LANES + a0 + tw))
    finish_part(G_PARTS - 2)
    g_tail("f", 1).wait_recv()

    @pl.loop(0, X_PARTS)
    def _(k):
        x_copy("y", k).wait_send()
        x_copy("c", k).wait_send()
        x_copy("f", k).wait_send()

    @pl.loop(0, G_PARTS)
    def _(k):
        g_copy("c", k).wait_send()

    @pl.loop(0, G_PARTS - 1)
    def _(k):
        g_copy("y", k).wait_send()
        g_copy("f", k).wait_send()

    for j in range(2):
        g_tail("y", j).wait_send()
        g_tail("f", j).wait_send()

    for i in range(1, n_chan):
        c_copy(i).wait_send()
    k_core().wait_send()
    k_across().wait_send()
    p_core_copy().wait_send()
    p_far_copy().wait_send()
    p_pass_copy().wait_send()
    for i in range(1, lines):
        k_line(i).wait_send()
    for i in range(lines):
        k_pair(i).wait_send()

    @pl.loop(1, n_dp)
    def _(i):
        s_copy(i).wait_send()
        a_copy(i).wait_send()
        f_copy(i).wait_send()


def tail_body(side, in_grad_vm, qf_vm, n_vm, g_vm, kt_vm, v_vm, in_grad_hbm, qf_hbm, err_hbm, v_tail, out, sem):
    n_chan, ch, cells = g_vm.shape
    channels = n_vm.shape[2]
    gw = cells // G_PARTS // 2
    done = cells - 2 * gw
    copies = [
        pltpu.make_async_copy(n_vm.at[t], err_hbm.at[0, :, pl.ds(t * channels, channels)], sem.at[t])
        for t in range(TAPS)
    ]
    copies.append(pltpu.make_async_copy(qf_vm, qf_hbm, sem.at[TAPS]))
    copies.append(pltpu.make_async_copy(in_grad_vm, in_grad_hbm.at[:, :done], sem.at[TAPS + 1]))
    for c in copies:
        c.start()
    v_tail[:, :, :LANES + gw] = v_vm[:, :, done:done + LANES + gw]
    v_tail[:, :, LANES + 2 * gw:] = jnp.zeros((3, ch, LANES), F32)
    tap_rows(side, kt_vm, g_vm[:, :, done + gw:].reshape(channels, gw), v_tail, slice(LANES + gw, LANES + 2 * gw))
    for k in range(2):
        out[:, k * gw:(k + 1) * gw] = finish_cells(side, v_tail, k * gw, gw)
    last = pltpu.make_async_copy(out, in_grad_hbm.at[:, done:], sem.at[TAPS + 2])
    last.start()
    for c in copies:
        c.wait()
    last.wait()


def per_device(activations, out_grad, kernel, error_in, q_prev):
    n_dp = lax.axis_size("dp")
    n_chan = lax.axis_size("chan")
    ch, cells = activations.shape
    channels = kernel.shape[1] // TAPS
    rank = q_prev.shape[1]
    side = round(cells ** 0.5)
    gw = cells // G_PARTS
    tiles = channels * TAPS // LANES
    pieces = -(-tiles // n_dp)
    packs = -(-pieces // (SUB // rank))
    kw = -(-TAPS * ch // LANES) * LANES
    fw = -(-ch // LANES) * LANES
    qt = q_prev.T
    p_rows = -(-TAPS * rank // (2 * SUB)) * 2 * SUB
    dma = pltpu.SemaphoreType.DMA
    anyspace = pl.BlockSpec(memory_space=pl.ANY)
    vmem = pl.BlockSpec(memory_space=pltpu.VMEM)
    held = pl.pallas_call(
        functools.partial(kernel_body, (n_dp, n_chan, side, rank, pieces)),
        out_shape=(
            pltpu.VMEM((ch, cells - gw), BF16),
            pltpu.VMEM((rank, ch), F32),
            pltpu.VMEM((TAPS, ch, channels), F32),
            pltpu.VMEM((n_chan, ch, cells), BF16),
            pltpu.VMEM((kw, channels), BF16),
            pltpu.VMEM((3, ch, cells + 2 * LANES), F32),
        ),
        in_specs=[anyspace, anyspace, anyspace, anyspace, vmem],
        out_specs=(vmem,) * 6,
        scratch_shapes=[
            pltpu.VMEM((n_chan, ch, cells), BF16),
            pltpu.VMEM((TAPS, ch, cells), BF16),
            pltpu.VMEM((TAPS, ch, channels), F32),
            pltpu.VMEM(kernel.shape, BF16),
            pltpu.VMEM((n_chan, ch, kw), BF16),
            pltpu.VMEM((n_chan, ch, kw), BF16),
            pltpu.VMEM((n_dp, packs, SUB, LANES), F32),
            pltpu.VMEM((n_dp, packs, SUB, LANES), F32),
            pltpu.VMEM((packs, SUB, LANES), F32),
            pltpu.VMEM((n_chan, packs, SUB, LANES), F32),
            pltpu.VMEM((n_dp, packs, SUB, LANES), F32),
            pltpu.VMEM((n_dp, packs, SUB, LANES), F32),
            pltpu.VMEM((n_dp, SUB, fw), F32),
            pltpu.VMEM((rank, ch, LANES), F32),
            pltpu.VMEM((2 * rank, cells // 2), F32),
            pltpu.VMEM((2 * rank, cells // 2), F32),
            pltpu.VMEM((2 * rank, cells // 4), F32),
            pltpu.VMEM((2, 2 * rank, cells // 4), F32),
            pltpu.VMEM((p_rows, cells), F32),
            pltpu.VMEM((3 * p_rows, ch), F32),
            pltpu.VMEM((TAPS, SUB, channels), F32),
            dma((3 + TAPS,)),
        ]
        + [dma((X_PARTS,))] * 6
        + [dma((G_PARTS + 1,))] * 6
        + [dma((n_chan - 1,))] * 4
        + [dma((n_dp - 1,))] * 2
        + [dma((n_chan - 1,))] * 2
        + [dma((n_dp - 1,))] * 4
        + [dma((GROUP - 1,))] * 2
        + [pltpu.SemaphoreType.REGULAR] * 2,
        compiler_params=pltpu.CompilerParams(
            collective_id=0, has_side_effects=True, vmem_limit_bytes=42000000
        ),
    )(activations, out_grad, kernel, error_in, qt)
    in_grad, qf_t, new_error = pl.pallas_call(
        functools.partial(tail_body, side),
        out_shape=(
            jax.ShapeDtypeStruct((ch, cells), BF16),
            jax.ShapeDtypeStruct((rank, ch), F32),
            jax.ShapeDtypeStruct(error_in.shape, F32),
        ),
        in_specs=[vmem] * 6,
        out_specs=(anyspace, anyspace, anyspace),
        scratch_shapes=[
            pltpu.VMEM((3, ch, gw + 2 * LANES), F32),
            pltpu.VMEM((ch, gw), BF16),
            dma((TAPS + 3,)),
        ],
        compiler_params=pltpu.CompilerParams(vmem_limit_bytes=12000000),
    )(*held)
    return in_grad, qf_t.T, new_error


def solution(mesh):
    in_specs = (
        P("chan", "dp"),
        P("chan", "dp"),
        P("chan", None),
        P("dp", "chan", None),
        P("chan", None),
    )
    out_specs = (P("chan", "dp"), P("chan", None), P("dp", "chan", None))
    return jax.shard_map(
        per_device, mesh=mesh, in_specs=in_specs, out_specs=out_specs, check_vma=False
    )
```

```python
import functools

import jax
import jax.numpy as jnp
from jax import lax
from jax.experimental import pallas as pl
from jax.experimental.pallas import tpu as pltpu
from jax.sharding import PartitionSpec as P

TAPS = 9
LANES = 128
SUB = 8
X_PARTS = 8
G_PARTS = 8
N_FIRST = 1
N_SECOND = 2
N_THIRD = 5
GROUP = 8
G_SPLIT = 3
HI = lax.Precision.HIGHEST
F32 = jnp.float32
BF16 = jnp.bfloat16


def tap_rows(side, kt, g_cols, v_buf, at):
    ch = v_buf.shape[1]
    gw = g_cols.shape[1]
    col = lax.broadcasted_iota(jnp.int32, (1, gw), 1) % side
    for a in range(3):
        y = lax.dot_general(
            kt[3 * a * ch:(3 * a + 3) * ch, :], g_cols,
            (((1,), (0,)), ((), ())), preferred_element_type=F32,
        )
        left = pltpu.roll(jnp.where(col != 0, y[:ch], 0.0), gw - 1, 1)
        right = pltpu.roll(jnp.where(col != side - 1, y[2 * ch:], 0.0), 1, 1)
        v_buf[a, :, at] = left + y[ch:2 * ch] + right


def finish_cells(side, v_buf, base, gw):
    wide = gw + LANES
    up = pltpu.roll(v_buf[0, :, pl.ds(pl.multiple_of(base + LANES, LANES), wide)], wide - side, 1)[:, :gw]
    down = pltpu.roll(v_buf[2, :, pl.ds(pl.multiple_of(base, LANES), wide)], wide - (LANES - side), 1)[:, :gw]
    mid = v_buf[1, :, pl.ds(pl.multiple_of(base + LANES, LANES), gw)]
    return (up + mid + down).astype(BF16)


def kernel_body(
    dims,
    x_hbm, g_hbm, k_hbm, e_hbm, qt_ref,
    in_grad_ref, qf_ref, n_ref, g_all, kt, v_buf,
    x_all, stack, e_vm, k_vm, k_send, k_all,
    s_buf, s_in, share, share_in, s_full, b_ref, f_buf, wide_q,
    p_own, p_core, p_half, p_in, p_taps, p_acc, p_wide,
    local_sem, xs_y, xr_y, xs_c, xr_c, xs_f, xr_f,
    gs_y, gr_y, gs_c, gr_c, gs_f, gr_f, ks, kr, ps, pr,
    ss, sr, cs, cr, as_, ar, fs, fr, bs, br, here, go,
):
    n_dp, n_chan, side, rank, pieces = dims
    ch, cells = x_hbm.shape
    channels = ch * n_chan
    dp = lax.axis_index("dp")
    me = lax.axis_index("chan")
    core = me + 1 - 2 * lax.rem(me, 2)
    far = lax.rem(me + 2, n_chan)
    diag = lax.rem(core + 2, n_chan)
    tiles = channels * TAPS // LANES
    tap_tiles = channels // LANES
    per = SUB // rank

    def dp_peer(i):
        return lax.rem(dp + i, n_dp)

    def ch_peer(i):
        return lax.rem(me + i, n_chan)

    barrier = pltpu.get_barrier_semaphore()
    root = (dp == 0) & (me == 0)

    for i in range(1, n_chan):
        @pl.when((dp != 0) | (ch_peer(i) != 0))
        def _():
            pl.semaphore_signal(barrier, inc=1, device_id={"chan": ch_peer(i)}, device_id_type=pl.DeviceIdType.MESH)

    @pl.when(dp != 0)
    def _():
        pl.semaphore_signal(barrier, inc=1, device_id={"dp": 0, "chan": 0}, device_id_type=pl.DeviceIdType.MESH)

    def enter_group():
        @pl.when(jnp.logical_not(root))
        def _():
            pl.semaphore_wait(barrier, n_chan - 1)

            @pl.when(dp == 0)
            def _():
                pl.semaphore_signal(here, inc=1, device_id={"chan": 0}, device_id_type=pl.DeviceIdType.MESH)

        @pl.when(root)
        def _():
            pl.semaphore_wait(here, n_chan - 1)

    def release_all():
        @pl.when(root)
        def _():
            pl.semaphore_wait(barrier, n_chan * (n_dp - 1))

            @pl.loop(1, n_dp)
            def _(d):
                for j in range(n_chan):
                    pl.semaphore_signal(go, inc=1, device_id={"dp": d, "chan": j}, device_id_type=pl.DeviceIdType.MESH)

            for j in range(1, n_chan):
                pl.semaphore_signal(go, inc=1, device_id={"chan": j}, device_id_type=pl.DeviceIdType.MESH)

    def enter_all():
        @pl.when(jnp.logical_not(root))
        def _():
            pl.semaphore_wait(go, 1)

    def remote(src, dst, send, recv, where):
        return pltpu.make_async_remote_copy(
            src_ref=src, dst_ref=dst, send_sem=send, recv_sem=recv,
            device_id=where, device_id_type=pl.DeviceIdType.MESH,
        )

    local = [
        pltpu.make_async_copy(g_hbm, g_all.at[me], local_sem.at[0]),
        pltpu.make_async_copy(k_hbm, k_vm, local_sem.at[1]),
        pltpu.make_async_copy(x_hbm, x_all.at[me], local_sem.at[2]),
    ]
    for t in range(TAPS):
        local.append(pltpu.make_async_copy(e_hbm.at[0, :, pl.ds(t * channels, channels)], e_vm.at[t], local_sem.at[3 + t]))
    for c in local:
        c.start()

    enter_group()

    xw = cells // X_PARTS
    gw = cells // G_PARTS

    def part(k, w):
        return pl.ds(pl.multiple_of(k * w, LANES), w)

    def x_copy(kind, k):
        s = part(k, xw)
        if kind == "y":
            return remote(x_hbm.at[:, s], x_all.at[me, :, s], xs_y.at[k], xr_y.at[k], {"chan": far})
        if kind == "c":
            return remote(x_hbm.at[:, s], x_all.at[me, :, s], xs_c.at[k], xr_c.at[k], {"chan": core})
        return remote(x_all.at[far, :, s], x_all.at[far, :, s], xs_f.at[k], xr_f.at[k], {"chan": core})

    def g_copy(kind, k, w=gw, at=None):
        s = part(k, w)
        at = k if at is None else at
        if kind == "y":
            return remote(g_hbm.at[:, s], g_all.at[me, :, s], gs_y.at[at], gr_y.at[at], {"chan": far})
        if kind == "c":
            return remote(g_hbm.at[:, s], g_all.at[me, :, s], gs_c.at[at], gr_c.at[at], {"chan": core})
        return remote(g_all.at[far, :, s], g_all.at[far, :, s], gs_f.at[at], gr_f.at[at], {"chan": core})

    def g_tail(kind, j):
        return g_copy(kind, 2 * (G_PARTS - 1) + j, gw // 2, G_PARTS - 1 + j)

    x_copy("y", 0).start()
    for k in range(X_PARTS):
        x_copy("c", k).start()

    def split3(v):
        high = v.astype(BF16)
        rest = v - high.astype(F32)
        mid = rest.astype(BF16)
        low = (rest - mid.astype(F32)).astype(BF16)
        return high, mid, low

    half = cells // 2
    quarter = cells // 4
    parity = lax.rem(me, 2)
    pad_r = jnp.zeros((SUB - rank, ch), F32)
    q_parts = [jnp.concatenate([v.astype(F32), pad_r], axis=0) for v in split3(qt_ref[...])]
    q_rows = jnp.concatenate(q_parts + [jnp.zeros((SUB, ch), F32)], axis=0).astype(BF16)
    local[0].wait()
    p = lax.dot_general(q_rows, g_all[me], (((1,), (0,)), ((), ())), preferred_element_type=F32)
    p = p[:SUB] + p[SUB:2 * SUB] + p[2 * SUB:3 * SUB]
    p_own[:rank, :] = p[:rank, :half]
    p_own[rank:, :] = p[:rank, half:]

    def p_core_copy():
        return remote(p_own, p_core, ps.at[0], pr.at[0], {"chan": core})

    def p_far_copy():
        return remote(p_half, p_in.at[parity], ps.at[1], pr.at[1], {"chan": far})

    def p_pass_copy():
        return remote(p_in.at[parity], p_in.at[parity], ps.at[2], pr.at[2], {"chan": core})

    p_core_copy().start()

    def spread(rows_t):
        pad_c = f_buf.shape[2] - ch
        square = jnp.concatenate([rows_t, jnp.zeros((rows_t.shape[0], pad_c), F32)], axis=1) if pad_c else rows_t
        square = jnp.concatenate([square, jnp.zeros((LANES - rows_t.shape[0], square.shape[1]), F32)], axis=0)
        turned = jnp.transpose(square)[:ch]
        for r in range(rank):
            wide_q[r] = jnp.broadcast_to(turned[:, r:r + 1], (ch, LANES))

    spread(qt_ref[...])
    p_core_copy().wait_recv()
    both = p_own[...] + p_core[...]
    p_half[...] = jnp.where(parity == 0, both[:, :quarter], both[:, quarter:])
    p_far_copy().start()
    x_copy("y", 1).start()
    for k in range(G_PARTS):
        g_copy("c", k).start()

    local[1].wait()
    for j in range(n_chan):
        for t in range(TAPS):
            k_send[j, :, t * ch:(t + 1) * ch] = k_vm[:, t * channels + j * ch:t * channels + (j + 1) * ch]
        k_send[j, :, TAPS * ch:] = jnp.zeros((ch, k_send.shape[2] - TAPS * ch), BF16)

    turn = lax.rem(dp, GROUP)
    first = dp - turn
    quarters = GROUP // 2
    lines = GROUP // 2
    line = turn // 2
    pair = lax.rem(turn, 2)
    k_width = k_send.shape[2] // quarters

    def k_piece(ln):
        owner = far + (diag - far) * (ln // (lines // 2))
        return owner, part(lax.rem(2 * ln + pair, quarters), k_width)

    across, k_lanes = k_piece(line)

    def k_core():
        return remote(k_send.at[core], k_all.at[me], ks.at[0], kr.at[0], {"chan": core})

    def k_across():
        return remote(k_send.at[across, :, k_lanes], k_all.at[me, :, k_lanes], ks.at[1], kr.at[1], {"chan": across})

    def k_line(i):
        block = k_all.at[across, :, k_lanes]
        peer = first + 2 * lax.rem(line + i, lines) + pair
        return remote(block, block, bs.at[i - 1], br.at[i - 1], {"dp": peer})

    def k_pair(i):
        owner, lanes = k_piece(lax.rem(line + lines - i, lines))
        block = k_all.at[owner, :, lanes]
        at = lines - 1 + i
        return remote(block, block, bs.at[at], br.at[at], {"dp": first + 2 * line + 1 - pair})

    k_across().start()
    x_copy("y", 2).start()
    k_core().start()
    rows = 16

    @pl.loop(0, ch // rows)
    def _(i):
        at = pl.ds(pl.multiple_of(i * rows, rows), rows)
        src = g_all[me, at, :].astype(F32)
        cell = lax.broadcasted_iota(jnp.int32, (1, cells), 1)
        col = cell % side
        row = cell // side
        for b in range(3):
            if b == 0:
                h = pltpu.roll(jnp.where(col != 0, src, 0.0), cells - 1, 1)
            elif b == 2:
                h = pltpu.roll(jnp.where(col != side - 1, src, 0.0), 1, 1)
            else:
                h = src
            for a in range(3):
                if a == 0:
                    v = pltpu.roll(jnp.where(row != 0, h, 0.0), cells - side, 1)
                elif a == 2:
                    v = pltpu.roll(jnp.where(row != side - 1, h, 0.0), side, 1)
                else:
                    v = h
                stack[3 * a + b, at, :] = v.astype(BF16)

    p_far_copy().wait_recv()
    p_pass_copy().start()
    release_all()
    x_copy("y", 3).start()
    k_all[me] = k_send[me]

    for a in range(3):
        v_buf[a, :, :LANES] = jnp.zeros((ch, LANES), F32)
        v_buf[a, :, LANES + cells:] = jnp.zeros((ch, LANES), F32)

    def place(at):
        piece = at % pieces
        return at // pieces, piece // per, piece % per * rank

    s_buf[...] = jnp.zeros(s_buf.shape, F32)
    for t in range(TAPS):
        local[3 + t].wait()
    for t in range(TAPS):
        for l in range(tap_tiles):
            at = t * tap_tiles + l
            value = e_vm[t, :, l * LANES:(l + 1) * LANES]
            sums = [
                jnp.sum(jnp.sum((value * wide_q[r]).reshape(ch // SUB, SUB, LANES), axis=0), axis=0, keepdims=True)
                for r in range(rank)
            ]
            o, c, r0 = place(at)
            s_buf[o, c, r0:r0 + rank, :] = jnp.concatenate(sums, axis=0)

    p_pass_copy().wait_recv()
    both = p_own[...] + p_core[...]
    both = jnp.concatenate([both[:, :quarter] + p_in[0], both[:, quarter:] + p_in[1]], axis=1)
    p = jnp.concatenate([both[:rank], both[rank:]], axis=1)
    cell = lax.broadcasted_iota(jnp.int32, (1, cells), 1)
    col = cell % side
    row = cell // side
    p_taps[TAPS * rank:] = jnp.zeros((p_taps.shape[0] - TAPS * rank, cells), F32)
    for b in range(3):
        if b == 0:
            h = pltpu.roll(jnp.where(col != 0, p, 0.0), cells - 1, 1)
        elif b == 2:
            h = pltpu.roll(jnp.where(col != side - 1, p, 0.0), 1, 1)
        else:
            h = p
        for a in range(3):
            if a == 0:
                v = pltpu.roll(jnp.where(row != 0, h, 0.0), cells - side, 1)
            elif a == 2:
                v = pltpu.roll(jnp.where(row != side - 1, h, 0.0), side, 1)
            else:
                v = h
            t = 3 * a + b
            p_taps[t * rank:(t + 1) * rank, :] = v

    local[2].wait()
    p_rows = p_taps.shape[0]
    p_acc[...] = jnp.zeros(p_acc.shape, F32)

    @pl.loop(0, X_PARTS)
    def _(k):
        s = part(k, xw)
        lhs = jnp.concatenate(split3(p_taps[:, s]), axis=0)
        p_acc[...] += lax.dot_general(lhs, x_all[me, :, s], (((1,), (1,)), ((), ())), preferred_element_type=F32)

    first_sketch = (p_acc[:p_rows] + p_acc[p_rows:2 * p_rows] + p_acc[2 * p_rows:]) * (1.0 / side)
    p_wide[...] = jnp.zeros(p_wide.shape, F32)
    for j in range(n_chan):
        @pl.when(me == j)
        def _():
            for t in range(TAPS):
                p_wide[t, :rank, j * ch:(j + 1) * ch] = first_sketch[t * rank:(t + 1) * rank]

    for t in range(TAPS):
        for l in range(tap_tiles):
            at = t * tap_tiles + l
            o, c, r0 = place(at)
            s_buf[o, c, r0:r0 + rank, :] += p_wide[t, :rank, l * LANES:(l + 1) * LANES]

    x_copy("y", 4).start()

    def forward_x(k):
        x_copy("y", k).wait_recv()
        x_copy("f", k).start()

    def run_n(first, last):
        @pl.loop(first, last)
        def _(k):
            @pl.when(k + 1 < X_PARTS)
            def _():
                forward_x(k + 1)

            x_copy("c", k).wait_recv()
            x_copy("f", k).wait_recv()
            s = part(k, xw)
            for a in range(3):
                lhs = stack[3 * a:3 * a + 3, :, s].reshape(3 * ch, xw)
                rhs = x_all[:, :, s].reshape(channels, xw)
                out = lax.dot_general(lhs, rhs, (((1,), (1,)), ((), ())), preferred_element_type=F32).reshape(3, ch, channels)

                @pl.when(k == 0)
                def _():
                    n_ref[3 * a:3 * a + 3] = out

                @pl.when(k > 0)
                def _():
                    n_ref[3 * a:3 * a + 3] += out

    def s_copy(i):
        peer = dp_peer(i)
        return remote(s_buf.at[peer], s_in.at[dp], ss.at[i - 1], sr.at[i - 1], {"dp": peer})

    enter_all()

    @pl.loop(1, n_dp)
    def _(i):
        s_copy(i).start()

    forward_x(0)
    run_n(0, N_FIRST)
    x_copy("y", 5).start()
    k_across().wait_recv()
    for i in range(1, lines):
        k_line(i).start()
    k_pair(0).start()

    def forward_g(k):
        g_copy("y", k).wait_recv()
        g_copy("f", k).start()

    def in_grad_arrived(k):
        g_copy("c", k).wait_recv()
        g_copy("f", k).wait_recv()

    def in_grad_part(k):
        in_grad_arrived(k)
        g_cols = g_all[:, :, part(k, gw)].reshape(channels, gw)
        tap_rows(side, kt, g_cols, v_buf, pl.ds(pl.multiple_of(LANES + k * gw, LANES), gw))

    def finish_part(k):
        in_grad_ref[:, part(k, gw)] = finish_cells(side, v_buf, k * gw, gw)

    def run_parts(begin, end):
        @pl.loop(begin, end)
        def _(k):
            @pl.when(k + 1 < G_PARTS - 1)
            def _():
                forward_g(k + 1)

            @pl.when(k + 1 == G_PARTS - 1)
            def _():
                g_tail("y", 0).wait_recv()
                g_tail("f", 0).start()

            in_grad_part(k)

            @pl.when(k > 0)
            def _():
                finish_part(k - 1)

    @pl.loop(1, n_dp)
    def _(i):
        s_copy(i).wait_recv()

    s_in[dp] = s_buf[dp]
    share[...] = lax.fori_loop(0, n_dp, lambda i, v: v + s_in[i], jnp.zeros(share.shape, F32))

    def c_copy(i):
        return remote(share, share_in.at[me], cs.at[i - 1], cr.at[i - 1], {"chan": ch_peer(i)})

    for i in range(1, n_chan):
        c_copy(i).start()
    share_in[me] = share[...]
    for k in range(6, X_PARTS):
        x_copy("y", k).start()
    for k in range(G_PARTS - 1):
        g_copy("y", k).start()
    for j in range(2):
        g_tail("y", j).start()
    run_n(N_FIRST, N_SECOND)
    for i in range(1, n_chan):
        c_copy(i).wait_recv()
    total = share_in[0]
    for i in range(1, n_chan):
        total = total + share_in[i]
    s_full[dp] = total * (1.0 / n_dp)

    def a_copy(i):
        return remote(s_full.at[dp], s_full.at[dp], as_.at[i - 1], ar.at[i - 1], {"dp": dp_peer(i)})

    @pl.loop(1, n_dp)
    def _(i):
        a_copy(i).start()

    run_n(N_SECOND, N_THIRD)

    @pl.loop(1, n_dp)
    def _(i):
        a_copy(i).wait_recv()

    cols = [[s_full[:, :, u * rank + r, :] for u in range(per)] for r in range(rank)]

    def inner(u, v):
        return sum(jnp.sum(x * y).reshape(1, 1, 1) for x, y in zip(u, v))

    gram = {}
    for i in range(rank):
        for j in range(i + 1):
            gram[i, j] = inner(cols[i], cols[j])
    low = {}
    for j in range(rank):
        d = gram[j, j]
        for m in range(j):
            d = d - low[j, m] * low[j, m]
        low[j, j] = jnp.sqrt(d)
        for i in range(j + 1, rank):
            d = gram[i, j]
            for m in range(j):
                d = d - low[i, m] * low[j, m]
            low[i, j] = d / low[j, j]
    base = []
    b_ref[...] = jnp.zeros(b_ref.shape, F32)
    for r in range(rank):
        v = cols[r]
        for m in range(r):
            v = [x - low[r, m] * y for x, y in zip(v, base[m])]
        v = [x / low[r, r] for x in v]
        base.append(v)
        for u in range(per):
            b_ref[:, :, u * rank + r, :] = v[u]

    for i in range(1, lines):
        k_line(i).wait_recv()
        k_pair(i).start()
    run_n(N_THIRD, X_PARTS)
    lane = lax.broadcasted_iota(jnp.int32, (1, LANES), 1)
    half = ch // 4
    blocks = []
    for h in range(ch // half):
        acc = [jnp.zeros((half, LANES), F32) for _ in range(rank)]
        for t in range(TAPS):
            for l in range(tap_tiles):
                at = t * tap_tiles + l
                rows_h = slice(h * half, (h + 1) * half)
                lanes = slice(l * LANES, (l + 1) * LANES)
                value = n_ref[t, rows_h, lanes] * (1.0 / side) + e_vm[t, rows_h, lanes]
                n_ref[t, rows_h, lanes] = value
                o, c, r0 = place(at)
                for r in range(rank):
                    acc[r] = acc[r] + value * b_ref[o, c, r0 + r:r0 + r + 1, :]
        block = jnp.zeros((half, LANES), F32)
        for r in range(rank):
            block = jnp.where(lane == r, jnp.sum(acc[r], axis=1, keepdims=True), block)
        blocks.append(block)
    pad_c = f_buf.shape[2] - ch
    if pad_c:
        blocks.append(jnp.zeros((pad_c, LANES), F32))
    f_buf[dp] = jnp.transpose(jnp.concatenate(blocks, axis=0))[:SUB]

    def f_copy(i):
        return remote(f_buf.at[dp], f_buf.at[dp], fs.at[i - 1], fr.at[i - 1], {"dp": dp_peer(i)})

    @pl.loop(1, n_dp)
    def _(i):
        f_copy(i).start()

    k_core().wait_recv()
    for i in range(lines):
        k_pair(i).wait_recv()
    for i in range(k_all.shape[2] // LANES):
        block = k_all[:, :, i * LANES:(i + 1) * LANES].reshape(channels, LANES)
        kt[i * LANES:(i + 1) * LANES, :] = jnp.transpose(block)

    forward_g(0)
    run_parts(0, G_SPLIT)

    @pl.loop(1, n_dp)
    def _(i):
        f_copy(i).wait_recv()

    fsum = lax.fori_loop(0, n_dp, lambda i, v: v + f_buf[i], jnp.zeros(f_buf.shape[1:], F32)) * (1.0 / n_dp)
    qf_ref[...] = fsum[:rank, :ch]
    spread(fsum[:rank, :ch])
    for t in range(TAPS):
        for l in range(tap_tiles):
            at = t * tap_tiles + l
            lanes = slice(l * LANES, (l + 1) * LANES)
            value = n_ref[t, :, lanes]
            o, c, r0 = place(at)
            for r in range(rank):
                value = value - wide_q[r] * b_ref[o, c, r0 + r:r0 + r + 1, :]
            n_ref[t, :, lanes] = value

    run_parts(G_SPLIT, G_PARTS - 1)
    g_tail("y", 1).wait_recv()
    g_tail("f", 1).start()
    g_copy("c", G_PARTS - 1).wait_recv()
    g_tail("f", 0).wait_recv()
    a0 = (G_PARTS - 1) * gw
    tw = gw // 2
    tap_rows(side, kt, g_all[:, :, a0:a0 + tw].reshape(channels, tw), v_buf, slice(LANES + a0, LANES + a0 + tw))
    finish_part(G_PARTS - 2)
    g_tail("f", 1).wait_recv()

    @pl.loop(0, X_PARTS)
    def _(k):
        x_copy("y", k).wait_send()
        x_copy("c", k).wait_send()
        x_copy("f", k).wait_send()

    @pl.loop(0, G_PARTS)
    def _(k):
        g_copy("c", k).wait_send()

    @pl.loop(0, G_PARTS - 1)
    def _(k):
        g_copy("y", k).wait_send()
        g_copy("f", k).wait_send()

    for j in range(2):
        g_tail("y", j).wait_send()
        g_tail("f", j).wait_send()

    for i in range(1, n_chan):
        c_copy(i).wait_send()
    k_core().wait_send()
    k_across().wait_send()
    p_core_copy().wait_send()
    p_far_copy().wait_send()
    p_pass_copy().wait_send()
    for i in range(1, lines):
        k_line(i).wait_send()
    for i in range(lines):
        k_pair(i).wait_send()

    @pl.loop(1, n_dp)
    def _(i):
        s_copy(i).wait_send()
        a_copy(i).wait_send()
        f_copy(i).wait_send()


def tail_body(side, in_grad_vm, qf_vm, n_vm, g_vm, kt_vm, v_vm, in_grad_hbm, qf_hbm, err_hbm, v_tail, out, sem):
    n_chan, ch, cells = g_vm.shape
    channels = n_vm.shape[2]
    gw = cells // G_PARTS // 2
    done = cells - 2 * gw
    copies = [
        pltpu.make_async_copy(n_vm.at[t], err_hbm.at[0, :, pl.ds(t * channels, channels)], sem.at[t])
        for t in range(TAPS)
    ]
    copies.append(pltpu.make_async_copy(qf_vm, qf_hbm, sem.at[TAPS]))
    copies.append(pltpu.make_async_copy(in_grad_vm, in_grad_hbm.at[:, :done], sem.at[TAPS + 1]))
    for c in copies:
        c.start()
    v_tail[:, :, :LANES + gw] = v_vm[:, :, done:done + LANES + gw]
    v_tail[:, :, LANES + 2 * gw:] = jnp.zeros((3, ch, LANES), F32)
    tap_rows(side, kt_vm, g_vm[:, :, done + gw:].reshape(channels, gw), v_tail, slice(LANES + gw, LANES + 2 * gw))
    for k in range(2):
        out[:, k * gw:(k + 1) * gw] = finish_cells(side, v_tail, k * gw, gw)
    last = pltpu.make_async_copy(out, in_grad_hbm.at[:, done:], sem.at[TAPS + 2])
    last.start()
    for c in copies:
        c.wait()
    last.wait()


def per_device(activations, out_grad, kernel, error_in, q_prev):
    n_dp = lax.axis_size("dp")
    n_chan = lax.axis_size("chan")
    ch, cells = activations.shape
    channels = kernel.shape[1] // TAPS
    rank = q_prev.shape[1]
    side = round(cells ** 0.5)
    gw = cells // G_PARTS
    tiles = channels * TAPS // LANES
    pieces = -(-tiles // n_dp)
    packs = -(-pieces // (SUB // rank))
    kw = -(-TAPS * ch // LANES) * LANES
    fw = -(-ch // LANES) * LANES
    qt = q_prev.T
    p_rows = -(-TAPS * rank // (2 * SUB)) * 2 * SUB
    dma = pltpu.SemaphoreType.DMA
    anyspace = pl.BlockSpec(memory_space=pl.ANY)
    vmem = pl.BlockSpec(memory_space=pltpu.VMEM)
    held = pl.pallas_call(
        functools.partial(kernel_body, (n_dp, n_chan, side, rank, pieces)),
        out_shape=(
            pltpu.VMEM((ch, cells - gw), BF16),
            pltpu.VMEM((rank, ch), F32),
            pltpu.VMEM((TAPS, ch, channels), F32),
            pltpu.VMEM((n_chan, ch, cells), BF16),
            pltpu.VMEM((kw, channels), BF16),
            pltpu.VMEM((3, ch, cells + 2 * LANES), F32),
        ),
        in_specs=[anyspace, anyspace, anyspace, anyspace, vmem],
        out_specs=(vmem,) * 6,
        scratch_shapes=[
            pltpu.VMEM((n_chan, ch, cells), BF16),
            pltpu.VMEM((TAPS, ch, cells), BF16),
            pltpu.VMEM((TAPS, ch, channels), F32),
            pltpu.VMEM(kernel.shape, BF16),
            pltpu.VMEM((n_chan, ch, kw), BF16),
            pltpu.VMEM((n_chan, ch, kw), BF16),
            pltpu.VMEM((n_dp, packs, SUB, LANES), F32),
            pltpu.VMEM((n_dp, packs, SUB, LANES), F32),
            pltpu.VMEM((packs, SUB, LANES), F32),
            pltpu.VMEM((n_chan, packs, SUB, LANES), F32),
            pltpu.VMEM((n_dp, packs, SUB, LANES), F32),
            pltpu.VMEM((n_dp, packs, SUB, LANES), F32),
            pltpu.VMEM((n_dp, SUB, fw), F32),
            pltpu.VMEM((rank, ch, LANES), F32),
            pltpu.VMEM((2 * rank, cells // 2), F32),
            pltpu.VMEM((2 * rank, cells // 2), F32),
            pltpu.VMEM((2 * rank, cells // 4), F32),
            pltpu.VMEM((2, 2 * rank, cells // 4), F32),
            pltpu.VMEM((p_rows, cells), F32),
            pltpu.VMEM((3 * p_rows, ch), F32),
            pltpu.VMEM((TAPS, SUB, channels), F32),
            dma((3 + TAPS,)),
        ]
        + [dma((X_PARTS,))] * 6
        + [dma((G_PARTS + 1,))] * 6
        + [dma((n_chan - 1,))] * 4
        + [dma((n_dp - 1,))] * 2
        + [dma((n_chan - 1,))] * 2
        + [dma((n_dp - 1,))] * 4
        + [dma((GROUP - 1,))] * 2
        + [pltpu.SemaphoreType.REGULAR] * 2,
        compiler_params=pltpu.CompilerParams(
            collective_id=0, has_side_effects=True, vmem_limit_bytes=42000000
        ),
    )(activations, out_grad, kernel, error_in, qt)
    in_grad, qf_t, new_error = pl.pallas_call(
        functools.partial(tail_body, side),
        out_shape=(
            jax.ShapeDtypeStruct((ch, cells), BF16),
            jax.ShapeDtypeStruct((rank, ch), F32),
            jax.ShapeDtypeStruct(error_in.shape, F32),
        ),
        in_specs=[vmem] * 6,
        out_specs=(anyspace, anyspace, anyspace),
        scratch_shapes=[
            pltpu.VMEM((3, ch, gw + 2 * LANES), F32),
            pltpu.VMEM((ch, gw), BF16),
            dma((TAPS + 3,)),
        ],
        compiler_params=pltpu.CompilerParams(vmem_limit_bytes=12000000),
    )(*held)
    return in_grad, qf_t.T, new_error


def solution(mesh):
    in_specs = (
        P("chan", "dp"),
        P("chan", "dp"),
        P("chan", None),
        P("dp", "chan", None),
        P("chan", None),
    )
    out_specs = (P("chan", "dp"), P("chan", None), P("dp", "chan", None))
    return jax.shard_map(
        per_device, mesh=mesh, in_specs=in_specs, out_specs=out_specs, check_vma=False
    )
```
